512 devices in a mesh: head: 16 (over x, z_lo), ctx: 32 (over y, z_hi, core).
Axes of the slice: x: 4, y: 8, z: 8 (z_hi: 2, z_lo: 4; z = z_hi * 4 + z_lo), core: 2. Of those that a mesh axis runs over, the one named last changes fastest.
Arguments:
- queries: bfloat16 [64, 128, 2048], P('ctx', 'head'), may hold values from -8 to 8
- key_vectors: bfloat16 [64, 128, 256], P('ctx', 'head'), may hold values from -8 to 8
- value_vectors: bfloat16 [64, 128, 256], P('ctx', 'head'), may hold values from -4 to 4
- out_grad: bfloat16 [64, 128, 2048], P('ctx', 'head'), may hold values from -4 to 4
- block_order: int32 [64], replicated, may hold values from 0 to 63, each once
Outputs:
- attended: bfloat16 [64, 128, 2048], P('ctx', 'head')
- query_grad: bfloat16 [64, 128, 2048], P('ctx', 'head')
- key_grad: bfloat16 [64, 128, 256], P('ctx', 'head')
- value_grad: bfloat16 [64, 128, 256], P('ctx', 'head')
The draws below stay inside these ranges and needn't reach their ends.
All inputs are finite; a program needn't handle non-finite values.
Results may differ from the reference program's by a relative error of at most 0.025.
Values may be sent and summed in bfloat16 or wider, within the bound.
A program may use at most 64 MiB of HBM per device.

```python
import math
import jax
import jax.numpy as jnp
from jax import lax

HD = 128
QH = 16
KVH = 2
BLOCK = 128
GROUP = 8
NBLOCK = 64


def draw_queries(key, part):
    normal_rows = jax.random.normal(jax.random.fold_in(key, 1), (NBLOCK, BLOCK, QH, HD), jnp.float32)
    entries = jnp.clip(normal_rows, -4.0, 4.0)
    return entries.reshape(NBLOCK, BLOCK, QH * HD).astype(jnp.bfloat16)


def draw_key_vectors(key, part):
    normal_rows = jax.random.normal(jax.random.fold_in(key, 3), (NBLOCK, BLOCK, KVH, HD), jnp.float32)
    entries = jnp.clip(normal_rows, -4.0, 4.0)
    return entries.reshape(NBLOCK, BLOCK, KVH * HD).astype(jnp.bfloat16)


def block_levels(key, shape, shards, low, top_value):
    gain, own = 1.0, jax.random.fold_in(key, 6)
    for position, blocks in shards:
        heights = jnp.exp(jax.random.uniform(jax.random.fold_in(own, position), (blocks,), jnp.float32, low / len(shards), top_value / len(shards)))
        gain = gain * jnp.repeat(heights, shape[position] // blocks).reshape([-1 if axis == position else 1 for axis in range(len(shape))])
    return gain


def noise(own_key, extent, deviation, limit, cuts=(), held_as=jnp.bfloat16):
    values = deviation * jax.random.normal(own_key, extent, jnp.float32)
    if cuts:
        values = values * block_levels(own_key, extent, cuts, -0.22, 0.18)
    return jnp.clip(values, -limit, limit).astype(held_as)


def setup_inputs(seed: int = 0) -> dict:
    splits = jax.random.split(jax.random.key(seed), 6)
    queries = draw_queries(jax.random.fold_in(splits[5], 71), 0)
    key_vectors = draw_key_vectors(jax.random.fold_in(splits[5], 71), 0)
    value_vectors = noise(splits[2], (NBLOCK, BLOCK, KVH * HD), 1.0, 4.0, ((0, 32), (1, 16)))
    out_grad = noise(splits[3], (NBLOCK, BLOCK, QH * HD), 1.0, 4.0, ((0, 32), (1, 16)))
    block_order = jax.random.permutation(splits[4], NBLOCK).astype(jnp.int32)
    return dict(queries=queries, key_vectors=key_vectors, value_vectors=value_vectors, out_grad=out_grad, block_order=block_order)


def head_pass(head_inputs, positions, scaling):
    query_rows, key_rows, value_rows, grad_rows = head_inputs
    tokens = query_rows.shape[0]
    tile_rows = 2 * BLOCK
    tile_count = tokens // tile_rows
    query_tiles = query_rows.reshape(tile_count, tile_rows, HD)
    grad_tiles = grad_rows.reshape(tile_count, tile_rows, HD)
    pos_tiles = positions.reshape(tile_count, tile_rows)

    def tile_step(totals, tile_inputs):
        key_total, value_total = totals
        query_tile, grad_tile, pos_tile = tile_inputs
        scores = jnp.dot(query_tile, key_rows.T, preferred_element_type=jnp.float32) * scaling
        allowed = positions[None, :] <= pos_tile[:, None]
        row_max = lax.optimization_barrier(jnp.max(jnp.where(allowed, scores, -jnp.inf), axis=1))
        row_sum = lax.optimization_barrier(jnp.sum(jnp.where(allowed, jnp.exp(scores - row_max[:, None]), 0.0), axis=1))
        log_total = row_max + jnp.log(row_sum)
        probs = jnp.where(allowed, jnp.exp(scores - log_total[:, None]), 0.0)
        weights = probs.astype(jnp.bfloat16)
        attended = jnp.dot(weights, value_rows, preferred_element_type=jnp.float32).astype(jnp.bfloat16)
        attended_wide = lax.optimization_barrier(attended).astype(jnp.float32)
        row_delta = lax.optimization_barrier(jnp.sum(grad_tile.astype(jnp.float32) * attended_wide, axis=1))
        grad_weights = jnp.dot(grad_tile, value_rows.T, preferred_element_type=jnp.float32)
        grad_scores = (probs * (grad_weights - row_delta[:, None])).astype(jnp.bfloat16)
        query_grad = (jnp.dot(grad_scores, key_rows, preferred_element_type=jnp.float32) * scaling).astype(jnp.bfloat16)
        key_total = key_total + jnp.dot(grad_scores.T, query_tile, preferred_element_type=jnp.float32)
        value_total = value_total + jnp.dot(weights.T, grad_tile, preferred_element_type=jnp.float32)
        return ((key_total, value_total), (attended, query_grad))
    empty_rows = jnp.zeros((tokens, HD), jnp.float32)
    totals, results = lax.scan(tile_step, (empty_rows, empty_rows), (query_tiles, grad_tiles, pos_tiles))
    attended = results[0].reshape(tokens, HD)
    query_grad = results[1].reshape(tokens, HD)
    return (attended, query_grad, totals[0], totals[1])

def reference(queries, key_vectors, value_vectors, out_grad, block_order):
    tokens = NBLOCK * BLOCK
    scaling = 1.0 / math.sqrt(HD)
    offsets = jnp.arange(BLOCK, dtype=jnp.int32)
    positions = (block_order.astype(jnp.int32)[:, None] * BLOCK + offsets[None, :]).reshape(tokens).astype(jnp.int32)
    query_heads = jnp.transpose(queries.reshape(tokens, QH, HD), (1, 0, 2))
    grad_heads = jnp.transpose(out_grad.reshape(tokens, QH, HD), (1, 0, 2))
    key_heads = jnp.repeat(jnp.transpose(key_vectors.reshape(tokens, KVH, HD), (1, 0, 2)), GROUP, axis=0)
    value_heads = jnp.repeat(jnp.transpose(value_vectors.reshape(tokens, KVH, HD), (1, 0, 2)), GROUP, axis=0)
    attended, query_grad, key_total, value_total = lax.map(lambda inputs: head_pass(inputs, positions, scaling), (query_heads, key_heads, value_heads, grad_heads))
    attended = jnp.transpose(attended, (1, 0, 2)).reshape(NBLOCK, BLOCK, QH * HD)
    query_grad = jnp.transpose(query_grad, (1, 0, 2)).reshape(NBLOCK, BLOCK, QH * HD)
    key_grad = (lax.optimization_barrier(jnp.sum(key_total.reshape(KVH, GROUP, tokens, HD), axis=1)) * scaling).astype(jnp.bfloat16)
    value_grad = lax.optimization_barrier(jnp.sum(value_total.reshape(KVH, GROUP, tokens, HD), axis=1)).astype(jnp.bfloat16)
    key_grad = jnp.transpose(key_grad, (1, 0, 2)).reshape(NBLOCK, BLOCK, KVH * HD)
    value_grad = jnp.transpose(value_grad, (1, 0, 2)).reshape(NBLOCK, BLOCK, KVH * HD)
    return (attended, query_grad, key_grad, value_grad)
```

```python
import functools
import math

import jax
import jax.numpy as jnp
from jax import lax
from jax.experimental import pallas as pl
from jax.experimental.pallas import tpu as pltpu
from jax.sharding import PartitionSpec as P

HD = 128
GROUP = 8
ROWS = 8
LOWEST = -1e30
MESH = pl.DeviceIdType.MESH
F32 = jnp.float32
BF16 = jnp.bfloat16

SPLIT = dict(x=4, z_lo=4, y=8, z_hi=2)
AHEAD = 3


def matmul(left_side, right_side):
    return lax.dot_general(
        left_side, right_side, (((1,), (0,)), ((), ())), preferred_element_type=F32
    )


def kernel(
    split,
    query_ref, grad_ref, key_ref, value_ref, order_ref,
    attended_out, query_out, key_out, value_out,
    query_all, grad_all, kv_all,
    query_rows, grad_rows, query_cols, grad_cols, key_cols, value_cols,
    key_pos, exps, grad_weights,
    max_rows, sum_rows, dot_rows, ratio_rows, delta_row, stat_all,
    attended_acc, query_acc, out_part, out_in,
    kv_part, sibling_in, y_send, y_in, z_send, z_in,
    q_ss, q_rs, z_ss, z_rs, ring_ss, ring_rs, sib_ss, sib_rs, stat_ss, stat_rs,
    dsib_ss, dsib_rs, dy_ss, dy_rs, dz_ss, dz_rs, out_ss, out_rs, local_sem,
):
    xs, zls, ys, zhs = split["x"], split["z_lo"], split["y"], split["z_hi"]
    zs, srcs = zls * zhs, 2 * xs
    toks = srcs * 2 * ROWS
    cols = GROUP * toks
    keys = 2 * zs * 2 * ROWS
    width = GROUP * HD
    block_len = xs * zls * ROWS
    step = min(256, cols)
    scaling = 1.0 / math.sqrt(HD)
    exp_scale = scaling / math.log(2.0)

    head, ctx = lax.axis_index("head"), lax.axis_index("ctx")
    x, zl = lax.div(head, zls), lax.rem(head, zls)
    core = lax.rem(ctx, 2)
    zh = lax.rem(lax.div(ctx, 2), zhs)
    y = lax.div(ctx, 2 * zhs)
    z = zh * zls + zl
    parity = lax.rem(zl, 2)
    me = x * 2 + parity

    def at(x_to, y_to, z_to, core_to):
        zh_to, zl_to = lax.div(z_to, zls), lax.rem(z_to, zls)
        return {"head": x_to * zls + zl_to, "ctx": (y_to * zhs + zh_to) * 2 + core_to}

    def source(index):
        return at(lax.div(index, 2), y, z - parity + lax.rem(index, 2), core)

    sibling = at(x, y, z, 1 - core)

    def remote(src, dst, send, recv, device):
        return pltpu.make_async_remote_copy(
            src_ref=src, dst_ref=dst, send_sem=send, recv_sem=recv,
            device_id=device, device_id_type=MESH,
        )

    def y_of(order):
        odd = lax.rem(order, 2)
        return lax.rem(
            y + odd * (ys - lax.div(order + 1, 2)) + (1 - odd) * lax.div(order, 2), ys
        )

    barrier = pltpu.get_barrier_semaphore()
    greeted = 1
    pl.semaphore_signal(barrier, inc=1, device_id=sibling, device_id_type=MESH)
    for hop in range(1, srcs):
        other = lax.rem(me + hop, srcs)
        pl.semaphore_signal(barrier, inc=1, device_id=source(other), device_id_type=MESH)
        greeted += 1
    for hop in range(1, ys):
        device = at(x, lax.rem(y + hop, ys), z, core)
        pl.semaphore_signal(barrier, inc=1, device_id=device, device_id_type=MESH)
        greeted += 1
    pair = z - parity
    for hop in range(2, zs):
        device = at(x, y, lax.rem(pair + hop, zs), core)
        pl.semaphore_signal(barrier, inc=1, device_id=device, device_id_type=MESH)
        greeted += 1
    pl.semaphore_wait(barrier, greeted)

    def kv_copy(part, ref, peer, own_slot):
        lanes = pl.ds(pl.multiple_of(lax.rem(peer, 2) * HD, HD), HD)
        return remote(
            ref.at[:, :, lanes], kv_all.at[y, core, part, own_slot],
            z_ss.at[part, peer], z_rs.at[part, own_slot], at(x, y, peer, core),
        )

    def query_copy(part, ref, dst, peer, own_slot):
        lanes = pl.ds(pl.multiple_of(lax.rem(peer, 2) * width, HD), width)
        return remote(
            ref.at[:, :, lanes], dst.at[own_slot],
            q_ss.at[part, peer], q_rs.at[part, own_slot], source(peer),
        )

    kv_refs = (key_ref, value_ref)
    query_refs = ((query_ref, query_all), (grad_ref, grad_all))
    for hop in range(1, zs):
        for part in range(2):
            kv_copy(part, kv_refs[part], lax.rem(z + hop, zs), z).start()
    for hop in range(1, srcs):
        for part in range(2):
            ref, dst = query_refs[part]
            query_copy(part, ref, dst, lax.rem(me + hop, srcs), me).start()
    own = []
    for part in range(2):
        lanes = pl.ds(pl.multiple_of(parity * HD, HD), HD)
        own.append(pltpu.make_async_copy(
            kv_refs[part].at[:, :, lanes], kv_all.at[y, core, part, z], local_sem.at[part]
        ))
        ref, dst = query_refs[part]
        lanes = pl.ds(pl.multiple_of(parity * width, HD), width)
        own.append(pltpu.make_async_copy(ref.at[:, :, lanes], dst.at[me], local_sem.at[2 + part]))
    for copy in own:
        copy.start()

    row_of = lax.broadcasted_iota(jnp.int32, (ROWS, toks), 0)

    def fill_positions(y_at, carry):
        for core_at in range(2):
            for z_at in range(zs):
                for half in range(2):
                    block = ((y_at * zhs + z_at // zls) * 2 + core_at) * 2 + half
                    first = order_ref[block] * block_len + (x * zls + z_at % zls) * ROWS
                    group = (core_at * zs + z_at) * 2 + half
                    key_pos[y_at, group * ROWS:(group + 1) * ROWS, :] = row_of + first
        return carry

    lax.fori_loop(0, ys, fill_positions, 0)
    token = lax.broadcasted_iota(jnp.int32, (1, toks), 1)
    half_of = lax.rem(lax.div(token, ROWS), 2)
    pair_of = lax.rem(lax.div(token, 2 * ROWS), 2)
    x_of = lax.div(token, 4 * ROWS)
    block_pos = jnp.where(half_of == 0, order_ref[ctx * 2], order_ref[ctx * 2 + 1])
    query_pos = (
        block_pos * block_len
        + (x_of * zls + (zl - parity) + pair_of) * ROWS
        + lax.rem(token, ROWS)
    )
    attended_acc[...] = jnp.zeros_like(attended_acc)
    query_acc[...] = jnp.zeros_like(query_acc)

    def ring_copy(order, to_order, to_right, send_slot):
        y_at = y_of(order)
        y_to = lax.rem(y + to_right + (1 - to_right) * (ys - 1), ys)
        return remote(
            kv_all.at[y_at, core], kv_all.at[y_at, core],
            ring_ss.at[send_slot], ring_rs.at[to_order], at(x, y_to, z, core),
        )

    def ring_arrival(order):
        y_at = y_of(order)
        return remote(
            kv_all.at[y_at, core], kv_all.at[y_at, core],
            ring_ss.at[order], ring_rs.at[order], sibling,
        )

    def sibling_copy(order, core_at):
        y_at = y_of(order)
        return remote(
            kv_all.at[y_at, core_at], kv_all.at[y_at, core_at],
            sib_ss.at[order], sib_rs.at[order], sibling,
        )

    def pass_on(order):
        ring_arrival(order).wait_recv()

        @pl.when(order + 2 < ys)
        def _():
            ring_copy(order, order + 2, lax.rem(order, 2), order).start()

        sibling_copy(order, core).start()

    for copy in own:
        copy.wait()
    for hop in range(1, zs):
        peer = lax.rem(z + hop, zs)
        for part in range(2):
            kv_copy(part, kv_refs[part], z, peer).wait_recv()
    ring_copy(0, 1, 1, ys - 1).start()
    if ys > 2:
        ring_copy(0, 2, 0, 0).start()
    sibling_copy(0, core).start()
    for order in range(1, min(AHEAD, ys)):
        pass_on(jnp.int32(order))
    for hop in range(1, srcs):
        peer = lax.rem(me + hop, srcs)
        for part in range(2):
            ref, dst = query_refs[part]
            query_copy(part, ref, dst, me, peer).wait_recv()
    for head_at in range(GROUP):
        lanes = slice(head_at * HD, (head_at + 1) * HD)
        rows = slice(head_at * toks, (head_at + 1) * toks)
        for src, by_row, by_col in (
            (query_all, query_rows, query_cols), (grad_all, grad_rows, grad_cols)
        ):
            tile = src[:, :, :, lanes].astype(F32).reshape(toks, HD)
            by_row[rows, :] = tile.astype(BF16)
            by_col[:, rows] = tile.T.astype(BF16)

    def forward(order, carry):
        @pl.when(order + AHEAD < ys)
        def _():
            pass_on(order + AHEAD)

        sibling_copy(order, 1 - core).wait_recv()
        y_at = y_of(order)
        key_wide = kv_all[y_at, :, 0].astype(F32).reshape(keys, HD)
        value_wide = kv_all[y_at, :, 1].astype(F32).reshape(keys, HD)
        key_cols[y_at] = key_wide.T.astype(BF16)
        value_cols[y_at] = value_wide.T.astype(BF16)
        key_tile, value_tile = key_wide.astype(BF16), value_wide.astype(BF16)
        allowed = jnp.concatenate([key_pos[y_at]] * (step // toks), axis=1) <= jnp.concatenate(
            [query_pos] * (step // toks), axis=1
        )
        for first in range(0, cols, step):
            lanes = slice(first, first + step)
            scores = jnp.where(allowed, matmul(key_tile, query_cols[:, lanes]), LOWEST)
            top = jnp.max(scores, axis=0, keepdims=True)
            exp_tile = jnp.exp2((scores - top) * exp_scale)
            weight_grad = matmul(value_tile, grad_cols[:, lanes])
            exps[y_at, :, lanes] = exp_tile
            grad_weights[y_at, :, lanes] = weight_grad
            max_rows[pl.ds(y_at, 1), lanes] = top
            sum_rows[pl.ds(y_at, 1), lanes] = jnp.sum(exp_tile, axis=0, keepdims=True)
            dot_rows[pl.ds(y_at, 1), lanes] = jnp.sum(
                exp_tile * weight_grad, axis=0, keepdims=True
            )
        return carry

    lax.fori_loop(0, ys, forward, 0)

    top = jnp.max(max_rows[...], axis=0, keepdims=True)
    factor = jnp.exp2((max_rows[...] - top) * exp_scale)
    stat_all[x] = jnp.concatenate(
        [
            top,
            jnp.sum(sum_rows[...] * factor, axis=0, keepdims=True),
            jnp.sum(dot_rows[...] * factor, axis=0, keepdims=True),
            jnp.zeros((5, cols), F32),
        ],
        axis=0,
    )

    def stat_copy(peer, own_slot):
        return remote(
            stat_all.at[own_slot], stat_all.at[own_slot],
            stat_ss.at[peer], stat_rs.at[own_slot], at(peer, y, z, core),
        )

    for hop in range(1, xs):
        stat_copy(lax.rem(x + hop, xs), x).start()
    for hop in range(1, xs):
        stat_copy(x, lax.rem(x + hop, xs)).wait_recv()
    tops = [stat_all[at_x, 0:1, :] for at_x in range(xs)]
    top = functools.reduce(jnp.maximum, tops)
    factors = [jnp.exp2((part - top) * exp_scale) for part in tops]
    total = sum(stat_all[at_x, 1:2, :] * factors[at_x] for at_x in range(xs))
    delta = sum(stat_all[at_x, 2:3, :] * factors[at_x] for at_x in range(xs)) / total
    delta_row[...] = delta
    ratio_rows[...] = jnp.exp2((max_rows[...] - top) * exp_scale) / total

    def dsib_copy(order, core_at):
        return remote(
            kv_part.at[order, core_at], sibling_in.at[order],
            dsib_ss.at[order], dsib_rs.at[order], sibling,
        )

    def dy_copy(order):
        return remote(
            y_send.at[order], y_in.at[order],
            dy_ss.at[order], dy_rs.at[order], at(x, y_of(order), z, core),
        )

    def send_sum(order):
        dsib_copy(order, 1 - core).wait_recv()
        y_send[order] = (
            kv_part[order, core].astype(F32) + sibling_in[order].astype(F32)
        ).astype(BF16)
        dy_copy(order).start()

    def backward(turn, carry):
        order = ys - 1 - turn
        y_at = y_of(order)
        key_sum = jnp.zeros((keys, HD), F32)
        value_sum = jnp.zeros((keys, HD), F32)
        for first in range(0, cols, step):
            lanes = slice(first, first + step)
            probs = exps[y_at, :, lanes] * ratio_rows[pl.ds(y_at, 1), lanes]
            weights = probs.astype(BF16)
            grad_scores = (
                probs * (grad_weights[y_at, :, lanes] - delta_row[:, lanes])
            ).astype(BF16)
            attended_acc[:, lanes] += matmul(value_cols[y_at], weights)
            query_acc[:, lanes] += matmul(key_cols[y_at], grad_scores)
            value_sum += matmul(weights, grad_rows[lanes, :])
            key_sum += matmul(grad_scores, query_rows[lanes, :])
        shape = (2, zs, 2, ROWS, HD)
        kv_part[order, :, 0] = (key_sum * scaling).reshape(shape).astype(BF16)
        kv_part[order, :, 1] = value_sum.reshape(shape).astype(BF16)
        dsib_copy(order, 1 - core).start()

        @pl.when(turn >= 1)
        def _():
            send_sum(order + 1)

        return carry

    lax.fori_loop(0, ys, backward, 0)

    for head_at in range(GROUP):
        lanes = slice(head_at * HD, (head_at + 1) * HD)
        rows = slice(head_at * toks, (head_at + 1) * toks)
        shape = (srcs, 2, ROWS, HD)
        out_part[:, 0, :, :, lanes] = attended_acc[:, rows].T.reshape(shape).astype(BF16)
        out_part[:, 1, :, :, lanes] = (
            (query_acc[:, rows] * scaling).T.reshape(shape).astype(BF16)
        )

    def out_copy(peer, own_slot):
        return remote(
            out_part.at[peer], out_in.at[own_slot],
            out_ss.at[peer], out_rs.at[own_slot], source(peer),
        )

    for hop in range(1, srcs):
        out_copy(lax.rem(me + hop, srcs), me).start()
    out_in[me] = out_part[me]

    dsib_copy(0, 1 - core).wait_recv()
    total_kv = kv_part[0, core].astype(F32) + sibling_in[0].astype(F32)
    for order in range(1, ys):
        dy_copy(order).wait_recv()
        total_kv += y_in[order].astype(F32)
    for part in range(2):
        z_send[:, part] = total_kv[part].astype(BF16)

    def dz_copy(peer, own_slot):
        return remote(
            z_send.at[peer], z_in.at[own_slot],
            dz_ss.at[peer], dz_rs.at[own_slot], at(x, y, peer, core),
        )

    for hop in range(1, zs):
        dz_copy(lax.rem(z + hop, zs), z).start()
    z_in[z] = z_send[z]
    for hop in range(1, srcs):
        out_copy(me, lax.rem(me + hop, srcs)).wait_recv()
    for half in range(2):
        lanes = slice(half * width, (half + 1) * width)
        for part, out in enumerate((attended_out, query_out)):
            out[:, :, lanes] = sum(
                out_in[at_x * 2 + half, part].astype(F32) for at_x in range(xs)
            ).astype(BF16)
    for hop in range(1, zs):
        dz_copy(z, lax.rem(z + hop, zs)).wait_recv()
    for half in range(2):
        lanes = slice(half * HD, (half + 1) * HD)
        for part, out in enumerate((key_out, value_out)):
            out[:, :, lanes] = sum(
                z_in[at_z, part].astype(F32) for at_z in range(half, zs, 2)
            ).astype(BF16)

    for hop in range(1, zs):
        peer = lax.rem(z + hop, zs)
        for part in range(2):
            kv_copy(part, kv_refs[part], peer, z).wait_send()
        dz_copy(peer, z).wait_send()
    for hop in range(1, srcs):
        peer = lax.rem(me + hop, srcs)
        for part in range(2):
            ref, dst = query_refs[part]
            query_copy(part, ref, dst, peer, me).wait_send()
        out_copy(peer, me).wait_send()
    for hop in range(1, xs):
        stat_copy(lax.rem(x + hop, xs), x).wait_send()
    ring_copy(0, 1, 1, ys - 1).wait_send()
    if ys > 2:
        ring_copy(0, 2, 0, 0).wait_send()
    for order in range(1, ys - 2):
        ring_copy(order, order + 2, order % 2, order).wait_send()
    for order in range(ys):
        sibling_copy(order, core).wait_send()
        dsib_copy(order, 1 - core).wait_send()
        if order:
            dy_copy(order).wait_send()


def shards(split, queries, key_vectors, value_vectors, out_grad, block_order):
    xs, zls, ys, zhs = split["x"], split["z_lo"], split["y"], split["z_hi"]
    zs, srcs = zls * zhs, 2 * xs
    toks = srcs * 2 * ROWS
    cols = GROUP * toks
    keys = 2 * zs * 2 * ROWS
    width = GROUP * HD
    vmem = pltpu.VMEM
    dma = pltpu.SemaphoreType.DMA
    kv_block = (2, zs, 2, ROWS, HD)
    whole = pl.BlockSpec(memory_space=pltpu.VMEM)
    return pl.pallas_call(
        functools.partial(kernel, split),
        out_shape=tuple(
            jax.ShapeDtypeStruct(a.shape, BF16)
            for a in (queries, queries, key_vectors, value_vectors)
        ),
        in_specs=[whole] * 4 + [pl.BlockSpec(memory_space=pltpu.SMEM)],
        out_specs=(whole,) * 4,
        scratch_shapes=[
            vmem((srcs, 2, ROWS, width), BF16), vmem((srcs, 2, ROWS, width), BF16),
            vmem((ys, 2) + kv_block, BF16),
            vmem((cols, HD), BF16), vmem((cols, HD), BF16),
            vmem((HD, cols), BF16), vmem((HD, cols), BF16),
            vmem((ys, HD, keys), BF16), vmem((ys, HD, keys), BF16),
            vmem((ys, keys, toks), jnp.int32),
            vmem((ys, keys, cols), F32), vmem((ys, keys, cols), F32),
            vmem((ys, cols), F32), vmem((ys, cols), F32), vmem((ys, cols), F32),
            vmem((ys, cols), F32), vmem((1, cols), F32), vmem((xs, 8, cols), F32),
            vmem((HD, cols), F32), vmem((HD, cols), F32),
            vmem((srcs, 2, 2, ROWS, width), BF16), vmem((srcs, 2, 2, ROWS, width), BF16),
            vmem((ys, 2) + kv_block, BF16), vmem((ys,) + kv_block, BF16),
            vmem((ys,) + kv_block, BF16), vmem((ys,) + kv_block, BF16),
            vmem((zs, 2, 2, ROWS, HD), BF16), vmem((zs, 2, 2, ROWS, HD), BF16),
            dma((2, srcs)), dma((2, srcs)), dma((2, zs)), dma((2, zs)),
            dma((ys,)), dma((ys,)), dma((ys,)), dma((ys,)), dma((xs,)), dma((xs,)),
            dma((ys,)), dma((ys,)), dma((ys,)), dma((ys,)),
            dma((zs,)), dma((zs,)), dma((srcs,)), dma((srcs,)), dma((4,)),
        ],
        compiler_params=pltpu.CompilerParams(
            collective_id=0, has_side_effects=True, vmem_limit_bytes=56 * 1024 * 1024
        ),
        name="attention",
    )(queries, out_grad, key_vectors, value_vectors, block_order)


def solution(mesh, split=SPLIT):
    rows = P("ctx", "head", None)
    return jax.shard_map(
        functools.partial(shards, split),
        mesh=mesh,
        in_specs=(rows, rows, rows, rows, P()),
        out_specs=(rows,) * 4,
        check_vma=False,
    )
```

```python
import functools
import math

import jax
import jax.numpy as jnp
from jax import lax
from jax.experimental import pallas as pl
from jax.experimental.pallas import tpu as pltpu
from jax.sharding import PartitionSpec as P

HD = 128
GROUP = 8
ROWS = 8
LOWEST = -1e30
MESH = pl.DeviceIdType.MESH
F32 = jnp.float32
BF16 = jnp.bfloat16

SPLIT = dict(x=4, z_lo=4, y=8, z_hi=2)


def matmul(left_side, right_side):
    return lax.dot_general(
        left_side, right_side, (((1,), (0,)), ((), ())), preferred_element_type=F32
    )


def kernel(
    split,
    query_ref, grad_ref, key_ref, value_ref, order_ref,
    attended_out, query_out, key_out, value_out,
    query_all, grad_all, key_all, value_all, value_stage,
    query_rows, grad_rows, query_cols, grad_cols, key_cols, value_cols,
    key_pos, exps, grad_weights,
    max_rows, sum_rows, dot_rows, ratio_rows, delta_row, stat_all,
    attended_acc, query_acc, out_part, out_in, pair_send, pair_in,
    kv_part, sibling_in, key_send, key_in, value_send, value_in,
    key_last, key_home, value_last, value_home,
    q_ss, q_rs, kz_ss, kz_rs, ky_ss, ky_rs, vy_ss, vy_rs, vz_ss, vz_rs,
    sk_ss, sk_rs, sv_ss, sv_rs, stat_ss, stat_rs, dsib_ss, dsib_rs,
    dky_ss, dky_rs, dkz_ss, dkz_rs, dvz_ss, dvz_rs, dvy_ss, dvy_rs,
    ox_ss, ox_rs, oz_ss, oz_rs, local_sem,
):
    xs, zls, ys, zhs = split["x"], split["z_lo"], split["y"], split["z_hi"]
    zs, srcs = zls * zhs, 2 * xs
    toks = srcs * 2 * ROWS
    cols = GROUP * toks
    keys = 2 * zs * 2 * ROWS
    width = GROUP * HD
    block_len = xs * zls * ROWS
    step = min(256, cols)
    half_ys = ys // 2
    scaling = 1.0 / math.sqrt(HD)
    exp_scale = scaling / math.log(2.0)

    head, ctx = lax.axis_index("head"), lax.axis_index("ctx")
    x, zl = lax.div(head, zls), lax.rem(head, zls)
    core = lax.rem(ctx, 2)
    zh = lax.rem(lax.div(ctx, 2), zhs)
    y = lax.div(ctx, 2 * zhs)
    z = zh * zls + zl
    parity = lax.rem(zl, 2)
    me, mate = x * 2 + parity, x * 2 + 1 - parity

    def at(x_to, y_to, z_to, core_to):
        zh_to, zl_to = lax.div(z_to, zls), lax.rem(z_to, zls)
        return {"head": x_to * zls + zl_to, "ctx": (y_to * zhs + zh_to) * 2 + core_to}

    def at_x(x_to):
        return at(x_to, y, z, core)

    def at_y(y_to):
        return at(x, y_to, z, core)

    def at_z(z_to):
        return at(x, y, z_to, core)

    sibling = at(x, y, z, 1 - core)
    mate_device = at_z(z + 1 - 2 * parity)

    def remote(src, dst, send, recv, device):
        return pltpu.make_async_remote_copy(
            src_ref=src, dst_ref=dst, send_sem=send, recv_sem=recv,
            device_id=device, device_id_type=MESH,
        )

    def nearest(own, order, size):
        odd = lax.rem(order, 2)
        return lax.rem(
            own + odd * (size - lax.div(order + 1, 2)) + (1 - odd) * lax.div(order, 2), size
        )

    def y_of(order):
        return nearest(y, order, ys)

    def z_of(order):
        return nearest(z, order, zs)

    def head_lanes(index, size):
        return pl.ds(pl.multiple_of(index * size, HD), size)

    barrier = pltpu.get_barrier_semaphore()
    greeted = [sibling]
    greeted += [at_x(lax.rem(x + hop, xs)) for hop in range(1, xs)]
    greeted += [at_y(lax.rem(y + hop, ys)) for hop in range(1, ys)]
    greeted += [at_z(lax.rem(z + hop, zs)) for hop in range(1, zs)]
    for device in greeted:
        pl.semaphore_signal(barrier, inc=1, device_id=device, device_id_type=MESH)
    pl.semaphore_wait(barrier, len(greeted))

    def key_z(peer, slot):
        return remote(
            key_ref.at[:, :, head_lanes(lax.rem(peer, 2), HD)], key_all.at[y, core, slot],
            kz_ss.at[peer], kz_rs.at[slot], at_z(peer),
        )

    def value_y(peer, slot):
        return remote(
            value_ref, value_stage.at[slot], vy_ss.at[peer], vy_rs.at[slot], at_y(peer)
        )

    query_refs = ((query_ref, query_all), (grad_ref, grad_all))

    def query_pair(part, slot):
        ref, dst = query_refs[part]
        return remote(
            ref.at[:, :, head_lanes(1 - parity, width)], dst.at[slot],
            q_ss.at[part, x], q_rs.at[part, slot], mate_device,
        )

    def query_own(part, x_to, slot):
        ref, dst = query_refs[part]
        return remote(
            ref.at[:, :, head_lanes(parity, width)], dst.at[slot],
            q_ss.at[part, x_to], q_rs.at[part, slot], at_x(x_to),
        )

    def query_mate(part, x_to, slot):
        dst = query_refs[part][1]
        return remote(
            dst.at[mate], dst.at[slot],
            q_ss.at[part, xs + x_to], q_rs.at[part, slot], at_x(x_to),
        )

    for order in range(1, zs):
        key_z(z_of(order), z).start()
    for order in range(1, ys):
        value_y(y_of(order), y).start()
    for part in range(2):
        query_pair(part, me).start()
    for part in range(2):
        for hop in range(1, xs):
            query_own(part, lax.rem(x + hop, xs), me).start()
    own = [
        pltpu.make_async_copy(
            key_ref.at[:, :, head_lanes(parity, HD)], key_all.at[y, core, z], local_sem.at[0]
        ),
        pltpu.make_async_copy(value_ref, value_stage.at[y], local_sem.at[1]),
    ]
    own += [
        pltpu.make_async_copy(
            ref.at[:, :, head_lanes(parity, width)], dst.at[me], local_sem.at[2 + part]
        )
        for part, (ref, dst) in enumerate(query_refs)
    ]
    for copy in own:
        copy.start()

    row_of = lax.broadcasted_iota(jnp.int32, (ROWS, toks), 0)

    def fill_positions(y_at, carry):
        for core_at in range(2):
            for z_at in range(zs):
                for half in range(2):
                    block = ((y_at * zhs + z_at // zls) * 2 + core_at) * 2 + half
                    first = order_ref[block] * block_len + (x * zls + z_at % zls) * ROWS
                    group = (core_at * zs + z_at) * 2 + half
                    key_pos[y_at, group * ROWS:(group + 1) * ROWS, :] = row_of + first
        return carry

    lax.fori_loop(0, ys, fill_positions, 0)
    token = lax.broadcasted_iota(jnp.int32, (1, toks), 1)
    half_of = lax.rem(lax.div(token, ROWS), 2)
    pair_of = lax.rem(lax.div(token, 2 * ROWS), 2)
    x_of = lax.div(token, 4 * ROWS)
    block_pos = jnp.where(half_of == 0, order_ref[ctx * 2], order_ref[ctx * 2 + 1])
    query_pos = (
        block_pos * block_len
        + (x_of * zls + (zl - parity) + pair_of) * ROWS
        + lax.rem(token, ROWS)
    )
    attended_acc[...] = jnp.zeros_like(attended_acc)
    query_acc[...] = jnp.zeros_like(query_acc)

    def key_y(peer, slot):
        return remote(
            key_all.at[slot, core], key_all.at[slot, core],
            ky_ss.at[peer], ky_rs.at[slot], at_y(peer),
        )

    def value_z(peer, slot):
        return remote(
            value_stage.at[:, :, :, head_lanes(lax.rem(peer, 2), HD)],
            value_all.at[:, core, slot], vz_ss.at[peer], vz_rs.at[slot], at_z(peer),
        )

    def key_sibling(y_at, core_at):
        ref = key_all.at[y_at, core_at]
        return remote(ref, ref, sk_ss.at[y_at], sk_rs.at[y_at], sibling)

    def value_sibling(z_at, core_at):
        ref = value_all.at[:, core_at, z_at]
        return remote(ref, ref, sv_ss.at[z_at], sv_rs.at[z_at], sibling)

    for copy in own:
        copy.wait()
    for order in range(1, zs):
        key_z(z, z_of(order)).wait_recv()
    for order in range(1, ys):
        key_y(y_of(order), y).start()
    key_sibling(y, core).start()
    for order in range(1, ys):
        value_y(y, y_of(order)).wait_recv()
    for order in range(1, zs):
        value_z(z_of(order), z).start()
    own_value = pltpu.make_async_copy(
        value_stage.at[:, :, :, head_lanes(parity, HD)], value_all.at[:, core, z],
        local_sem.at[4],
    )
    own_value.start()
    for part in range(2):
        query_pair(part, mate).wait_recv()
        for hop in range(1, xs):
            query_mate(part, lax.rem(x + hop, xs), mate).start()
    own_value.wait()
    value_sibling(z, core).start()
    for part in range(2):
        for hop in range(1, xs):
            other = lax.rem(x + hop, xs)
            query_own(part, x, other * 2 + parity).wait_recv()
            query_mate(part, x, other * 2 + 1 - parity).wait_recv()
    for head_at in range(GROUP):
        lanes = slice(head_at * HD, (head_at + 1) * HD)
        rows = slice(head_at * toks, (head_at + 1) * toks)
        for src, by_row, by_col in (
            (query_all, query_rows, query_cols), (grad_all, grad_rows, grad_cols)
        ):
            tile = src[:, :, :, lanes].astype(F32).reshape(toks, HD)
            by_row[rows, :] = tile.astype(BF16)
            by_col[:, rows] = tile.T.astype(BF16)

    def pass_key(order):
        y_at = y_of(order)
        key_y(y, y_at).wait_recv()
        key_sibling(y_at, core).start()

    def pass_value(order):
        z_at = z_of(order)
        value_z(z, z_at).wait_recv()
        value_sibling(z_at, core).start()

    def score(order, carry):
        @pl.when(order + 1 < ys)
        def _():
            pass_key(order + 1)

        @pl.when(order + 1 < zs)
        def _():
            pass_value(order + 1)

        y_at = y_of(order)
        key_sibling(y_at, 1 - core).wait_recv()
        key_wide = key_all[y_at].astype(F32).reshape(keys, HD)
        key_cols[y_at] = key_wide.T.astype(BF16)
        key_tile = key_wide.astype(BF16)
        allowed = jnp.concatenate([key_pos[y_at]] * (step // toks), axis=1) <= jnp.concatenate(
            [query_pos] * (step // toks), axis=1
        )
        for first in range(0, cols, step):
            lanes = slice(first, first + step)
            scores = jnp.where(allowed, matmul(key_tile, query_cols[:, lanes]), LOWEST)
            top = jnp.max(scores, axis=0, keepdims=True)
            exp_tile = jnp.exp2((scores - top) * exp_scale)
            exps[y_at, :, lanes] = exp_tile
            max_rows[pl.ds(y_at, 1), lanes] = top
            sum_rows[pl.ds(y_at, 1), lanes] = jnp.sum(exp_tile, axis=0, keepdims=True)
        return carry

    lax.fori_loop(0, ys, score, 0)
    for order in range(ys + 1, zs):
        pass_value(order)
    for order in range(zs):
        value_sibling(z_of(order), 1 - core).wait_recv()

    def weigh(y_at, carry):
        value_wide = value_all[y_at].astype(F32).reshape(keys, HD)
        value_cols[y_at] = value_wide.T.astype(BF16)
        value_tile = value_wide.astype(BF16)
        for first in range(0, cols, step):
            lanes = slice(first, first + step)
            weight_grad = matmul(value_tile, grad_cols[:, lanes])
            grad_weights[y_at, :, lanes] = weight_grad
            dot_rows[pl.ds(y_at, 1), lanes] = jnp.sum(
                exps[y_at, :, lanes] * weight_grad, axis=0, keepdims=True
            )
        return carry

    lax.fori_loop(0, ys, weigh, 0)

    top = jnp.max(max_rows[...], axis=0, keepdims=True)
    factor = jnp.exp2((max_rows[...] - top) * exp_scale)
    for index, row in enumerate((
        top,
        jnp.sum(sum_rows[...] * factor, axis=0, keepdims=True),
        jnp.sum(dot_rows[...] * factor, axis=0, keepdims=True),
    )):
        for head_at in range(GROUP):
            stat_all[x, index, head_at:head_at + 1, :] = row[
                :, head_at * toks:(head_at + 1) * toks
            ]

    def stat_copy(peer, slot):
        return remote(
            stat_all.at[slot], stat_all.at[slot], stat_ss.at[peer], stat_rs.at[slot], at_x(peer)
        )

    for hop in range(1, xs):
        stat_copy(lax.rem(x + hop, xs), x).start()
    for hop in range(1, xs):
        stat_copy(x, lax.rem(x + hop, xs)).wait_recv()
    tops = [stat_all[x_at, 0] for x_at in range(xs)]
    top = functools.reduce(jnp.maximum, tops)
    factors = [jnp.exp2((part - top) * exp_scale) for part in tops]
    total = sum(stat_all[x_at, 1] * factors[x_at] for x_at in range(xs))
    inverse = 1.0 / total
    delta = sum(stat_all[x_at, 2] * factors[x_at] for x_at in range(xs)) * inverse
    for head_at in range(GROUP):
        lanes = slice(head_at * toks, (head_at + 1) * toks)
        row = slice(head_at, head_at + 1)
        delta_row[:, lanes] = delta[row]
        ratio_rows[:, lanes] = (
            jnp.exp2((max_rows[:, lanes] - top[row]) * exp_scale) * inverse[row]
        )

    def dsib_copy(order, core_at):
        return remote(
            kv_part.at[order, core_at], sibling_in.at[order],
            dsib_ss.at[order], dsib_rs.at[order], sibling,
        )

    def dkey_y(order):
        return remote(
            key_send.at[order], key_in.at[order],
            dky_ss.at[order], dky_rs.at[order], at_y(y_of(order)),
        )

    def dvalue_z(batch, peer, slot):
        orders = pl.ds(batch * half_ys, half_ys)
        return remote(
            value_send.at[peer, orders], value_in.at[slot, orders],
            dvz_ss.at[batch, peer], dvz_rs.at[batch, slot], at_z(peer),
        )

    def add_sibling(order):
        dsib_copy(order, 1 - core).wait_recv()
        key_send[order] = (
            kv_part[order, core, 0].astype(F32) + sibling_in[order, 0].astype(F32)
        ).astype(BF16)
        value_send[:, order] = (
            kv_part[order, core, 1].astype(F32) + sibling_in[order, 1].astype(F32)
        ).astype(BF16)

    def backward(turn, carry):
        order = ys - 1 - turn
        y_at = y_of(order)
        key_sum = jnp.zeros((keys, HD), F32)
        value_sum = jnp.zeros((keys, HD), F32)
        for first in range(0, cols, step):
            lanes = slice(first, first + step)
            probs = exps[y_at, :, lanes] * ratio_rows[pl.ds(y_at, 1), lanes]
            weights = probs.astype(BF16)
            grad_scores = (
                probs * (grad_weights[y_at, :, lanes] - delta_row[:, lanes])
            ).astype(BF16)
            attended_acc[:, lanes] += matmul(value_cols[y_at], weights)
            query_acc[:, lanes] += matmul(key_cols[y_at], grad_scores)
            value_sum += matmul(weights, grad_rows[lanes, :])
            key_sum += matmul(grad_scores, query_rows[lanes, :])
        shape = (2, zs, 2, ROWS, HD)
        kv_part[order, :, 0] = (key_sum * scaling).reshape(shape).astype(BF16)
        kv_part[order, :, 1] = value_sum.reshape(shape).astype(BF16)
        dsib_copy(order, 1 - core).start()

        @pl.when(turn >= 1)
        def _():
            add_sibling(order + 1)
            dkey_y(order + 1).start()

        @pl.when(order + 1 == half_ys)
        def _():
            for near in range(1, zs):
                dvalue_z(1, z_of(near), z).start()

        return carry

    lax.fori_loop(0, ys, backward, 0)

    for head_at in range(GROUP):
        lanes = slice(head_at * HD, (head_at + 1) * HD)
        rows = slice(head_at * toks, (head_at + 1) * toks)
        shape = (xs, 2, 2, ROWS, HD)
        out_part[:, :, 0, :, :, lanes] = attended_acc[:, rows].T.reshape(shape).astype(BF16)
        out_part[:, :, 1, :, :, lanes] = (
            (query_acc[:, rows] * scaling).T.reshape(shape).astype(BF16)
        )

    def out_x(peer, slot):
        return remote(
            out_part.at[peer], out_in.at[slot], ox_ss.at[peer], ox_rs.at[slot], at_x(peer)
        )

    for hop in range(1, xs):
        out_x(lax.rem(x + hop, xs), x).start()
    add_sibling(0)
    for near in range(1, zs):
        dvalue_z(0, z_of(near), z).start()
    out_in[x] = out_part[x]
    value_in[z] = value_send[z]

    total_key = key_send[0].astype(F32)
    for order in range(1, ys):
        dkey_y(order).wait_recv()
        total_key += key_in[order].astype(F32)
    key_last[...] = total_key.astype(BF16)

    def dkey_z(peer, slot):
        return remote(
            key_last.at[peer], key_home.at[slot], dkz_ss.at[peer], dkz_rs.at[slot], at_z(peer)
        )

    def dvalue_y(order):
        return remote(
            value_last.at[order], value_home.at[order],
            dvy_ss.at[order], dvy_rs.at[order], at_y(y_of(order)),
        )

    for near in range(1, zs):
        dkey_z(z_of(near), z).start()
    key_home[z] = key_last[z]
    for near in range(1, zs):
        for batch in range(2):
            dvalue_z(batch, z, z_of(near)).wait_recv()
    for half in range(2):
        value_last[:, half] = sum(
            value_in[z_at].astype(F32) for z_at in range(half, zs, 2)
        ).astype(BF16)
    for order in range(1, ys):
        dvalue_y(order).start()
    value_home[0] = value_last[0]

    for hop in range(1, xs):
        out_x(x, lax.rem(x + hop, xs)).wait_recv()
    pair_send[...] = sum(
        out_in[x_at, 1 - parity].astype(F32) for x_at in range(xs)
    ).astype(BF16)
    pair_copy = remote(pair_send, pair_in, oz_ss.at[0], oz_rs.at[0], mate_device)
    pair_copy.start()
    mine = sum(out_in[x_at, parity].astype(F32) for x_at in range(xs)).astype(BF16)
    for part, out in enumerate((attended_out, query_out)):
        out[:, :, head_lanes(parity, width)] = mine[part]

    for near in range(1, zs):
        dkey_z(z, z_of(near)).wait_recv()
    for half in range(2):
        key_out[:, :, half * HD:(half + 1) * HD] = sum(
            key_home[z_at].astype(F32) for z_at in range(half, zs, 2)
        ).astype(BF16)
    for order in range(1, ys):
        dvalue_y(order).wait_recv()
    for half in range(2):
        value_out[:, :, half * HD:(half + 1) * HD] = sum(
            value_home[order, half].astype(F32) for order in range(ys)
        ).astype(BF16)
    pair_copy.wait_recv()
    for part, out in enumerate((attended_out, query_out)):
        out[:, :, head_lanes(1 - parity, width)] = pair_in[part]

    for order in range(zs):
        peer = z_of(order)
        value_sibling(peer, core).wait_send()
        if order:
            key_z(peer, z).wait_send()
            value_z(peer, z).wait_send()
            dkey_z(peer, z).wait_send()
            for batch in range(2):
                dvalue_z(batch, peer, z).wait_send()
    for order in range(ys):
        peer = y_of(order)
        key_sibling(peer, core).wait_send()
        dsib_copy(order, 1 - core).wait_send()
        if order:
            value_y(peer, y).wait_send()
            key_y(peer, y).wait_send()
            dkey_y(order).wait_send()
            dvalue_y(order).wait_send()
    for hop in range(1, xs):
        peer = lax.rem(x + hop, xs)
        for part in range(2):
            query_own(part, peer, me).wait_send()
            query_mate(part, peer, mate).wait_send()
        stat_copy(peer, x).wait_send()
        out_x(peer, x).wait_send()
    for part in range(2):
        query_pair(part, me).wait_send()
    pair_copy.wait_send()


def finish(*refs):
    for src, dst in zip(refs[:4], refs[4:]):
        dst[...] = src[...]


def shards(split, queries, key_vectors, value_vectors, out_grad, block_order):
    xs, zls, ys, zhs = split["x"], split["z_lo"], split["y"], split["z_hi"]
    zs, srcs = zls * zhs, 2 * xs
    toks = srcs * 2 * ROWS
    cols = GROUP * toks
    keys = 2 * zs * 2 * ROWS
    width = GROUP * HD
    vmem = pltpu.VMEM
    dma = pltpu.SemaphoreType.DMA
    tile = (2, ROWS, HD)
    whole = pl.BlockSpec(memory_space=pltpu.VMEM)
    results = tuple(
        jax.ShapeDtypeStruct(a.shape, BF16)
        for a in (queries, queries, key_vectors, value_vectors)
    )
    partial_sums = pl.pallas_call(
        functools.partial(kernel, split),
        out_shape=results,
        in_specs=[whole] * 4 + [pl.BlockSpec(memory_space=pltpu.SMEM)],
        out_specs=(whole,) * 4,
        scratch_shapes=[
            vmem((srcs, 2, ROWS, width), BF16), vmem((srcs, 2, ROWS, width), BF16),
            vmem((ys, 2, zs) + tile, BF16), vmem((ys, 2, zs) + tile, BF16),
            vmem((ys,) + value_vectors.shape, BF16),
            vmem((cols, HD), BF16), vmem((cols, HD), BF16),
            vmem((HD, cols), BF16), vmem((HD, cols), BF16),
            vmem((ys, HD, keys), BF16), vmem((ys, HD, keys), BF16),
            vmem((ys, keys, toks), jnp.int32),
            vmem((ys, keys, cols), F32), vmem((ys, keys, cols), F32),
            vmem((ys, cols), F32), vmem((ys, cols), F32), vmem((ys, cols), F32),
            vmem((ys, cols), F32), vmem((1, cols), F32), vmem((xs, 3, GROUP, toks), F32),
            vmem((HD, cols), F32), vmem((HD, cols), F32),
            vmem((xs, 2, 2, 2, ROWS, width), BF16), vmem((xs, 2, 2, 2, ROWS, width), BF16),
            vmem((2, 2, ROWS, width), BF16), vmem((2, 2, ROWS, width), BF16),
            vmem((ys, 2, 2, zs) + tile, BF16), vmem((ys, 2, zs) + tile, BF16),
            vmem((ys, zs) + tile, BF16), vmem((ys, zs) + tile, BF16),
            vmem((zs, ys) + tile, BF16), vmem((zs, ys) + tile, BF16),
            vmem((zs,) + tile, BF16), vmem((zs,) + tile, BF16),
            vmem((ys, 2) + tile, BF16), vmem((ys, 2) + tile, BF16),
            dma((2, 2 * xs)), dma((2, srcs)), dma((zs,)), dma((zs,)), dma((ys,)), dma((ys,)),
            dma((ys,)), dma((ys,)), dma((zs,)), dma((zs,)),
            dma((ys,)), dma((ys,)), dma((zs,)), dma((zs,)), dma((xs,)), dma((xs,)),
            dma((ys,)), dma((ys,)),
            dma((ys,)), dma((ys,)), dma((zs,)), dma((zs,)),
            dma((2, zs)), dma((2, zs)), dma((ys,)), dma((ys,)),
            dma((xs,)), dma((xs,)), dma((1,)), dma((1,)), dma((5,)),
        ],
        compiler_params=pltpu.CompilerParams(
            collective_id=0, has_side_effects=True, vmem_limit_bytes=56 * 1024 * 1024
        ),
        name="attention",
    )(queries, out_grad, key_vectors, value_vectors, block_order)
    return pl.pallas_call(
        finish, out_shape=results, in_specs=[whole] * 4, out_specs=(whole,) * 4, name="finish"
    )(*partial_sums)


def solution(mesh, split=SPLIT):
    rows = P("ctx", "head", None)
    return jax.shard_map(
        functools.partial(shards, split),
        mesh=mesh,
        in_specs=(rows, rows, rows, rows, P()),
        out_specs=(rows,) * 4,
        check_vma=False,
    )
```

```python
import functools
import math

import jax
import jax.numpy as jnp
from jax import lax
from jax.experimental import pallas as pl
from jax.experimental.pallas import tpu as pltpu
from jax.sharding import PartitionSpec as P

HD = 128
GROUP = 8
ROWS = 8
LOWEST = -1e30
MESH = pl.DeviceIdType.MESH
F32 = jnp.float32
BF16 = jnp.bfloat16

SPLIT = dict(x=4, z_lo=4, y=8, z_hi=2)


def matmul(left_side, right_side):
    return lax.dot_general(
        left_side, right_side, (((1,), (0,)), ((), ())), preferred_element_type=F32
    )


def kernel(
    split,
    query_ref, grad_ref, key_ref, value_ref, order_ref,
    attended_out, query_out, key_out, value_out,
    query_all, grad_all, key_all, value_all, value_stage,
    query_rows, grad_rows, query_cols, grad_cols, key_cols, value_cols,
    key_pos, exps, grad_weights,
    max_rows, sum_rows, dot_rows, ratio_rows, delta_row, scale_row, stat_all,
    attended_acc, query_acc, out_part, out_in, pair_send, pair_in,
    kv_part, sibling_in, key_send, key_in, value_send, value_in,
    key_last, key_home, value_last, value_home,
    q_ss, q_rs, kz_ss, kz_rs, ky_ss, ky_rs, vy_ss, vy_rs, vz_ss, vz_rs,
    sk_ss, sk_rs, sv_ss, sv_rs, stat_ss, stat_rs, dsib_ss, dsib_rs,
    dky_ss, dky_rs, dkz_ss, dkz_rs, dvz_ss, dvz_rs, dvy_ss, dvy_rs,
    ox_ss, ox_rs, oz_ss, oz_rs, local_sem,
):
    xs, zls, ys, zhs = split["x"], split["z_lo"], split["y"], split["z_hi"]
    zs, srcs = zls * zhs, 2 * xs
    toks = srcs * 2 * ROWS
    cols = GROUP * toks
    keys = 2 * zs * 2 * ROWS
    width = GROUP * HD
    block_len = xs * zls * ROWS
    step = min(256, cols)
    scaling = 1.0 / math.sqrt(HD)
    exp_scale = scaling / math.log(2.0)

    head, ctx = lax.axis_index("head"), lax.axis_index("ctx")
    x, zl = lax.div(head, zls), lax.rem(head, zls)
    core = lax.rem(ctx, 2)
    zh = lax.rem(lax.div(ctx, 2), zhs)
    y = lax.div(ctx, 2 * zhs)
    z = zh * zls + zl
    parity = lax.rem(zl, 2)
    me, mate = x * 2 + parity, x * 2 + 1 - parity

    def at(x_to, y_to, z_to, core_to):
        zh_to, zl_to = lax.div(z_to, zls), lax.rem(z_to, zls)
        return {"head": x_to * zls + zl_to, "ctx": (y_to * zhs + zh_to) * 2 + core_to}

    def at_x(x_to):
        return at(x_to, y, z, core)

    def at_y(y_to):
        return at(x, y_to, z, core)

    def at_z(z_to):
        return at(x, y, z_to, core)

    sibling = at(x, y, z, 1 - core)
    mate_device = at_z(z + 1 - 2 * parity)

    def remote(src, dst, send, recv, device):
        return pltpu.make_async_remote_copy(
            src_ref=src, dst_ref=dst, send_sem=send, recv_sem=recv,
            device_id=device, device_id_type=MESH,
        )

    def nearest(own, order, size):
        odd = lax.rem(order, 2)
        return lax.rem(
            own + odd * (size - lax.div(order + 1, 2)) + (1 - odd) * lax.div(order, 2), size
        )

    def y_of(order):
        return nearest(y, order, ys)

    def z_of(order):
        return nearest(z, order, zs)

    def head_lanes(index, size):
        return pl.ds(pl.multiple_of(index * size, HD), size)

    barrier = pltpu.get_barrier_semaphore()
    greeted = [sibling]
    greeted += [at_x(lax.rem(x + hop, xs)) for hop in range(1, xs)]
    greeted += [at_y(lax.rem(y + hop, ys)) for hop in range(1, ys)]
    greeted += [at_z(lax.rem(z + hop, zs)) for hop in range(1, zs)]
    for device in greeted:
        pl.semaphore_signal(barrier, inc=1, device_id=device, device_id_type=MESH)
    pl.semaphore_wait(barrier, len(greeted))

    def key_z(peer, slot):
        return remote(
            key_ref.at[:, :, head_lanes(lax.rem(peer, 2), HD)], key_all.at[y, core, slot],
            kz_ss.at[peer], kz_rs.at[slot], at_z(peer),
        )

    def value_y(peer, slot):
        return remote(
            value_ref, value_stage.at[slot], vy_ss.at[peer], vy_rs.at[slot], at_y(peer)
        )

    query_refs = ((query_ref, query_all), (grad_ref, grad_all))

    def query_pair(part, slot):
        ref, dst = query_refs[part]
        return remote(
            ref.at[:, :, head_lanes(1 - parity, width)], dst.at[slot],
            q_ss.at[part, x], q_rs.at[part, slot], mate_device,
        )

    def query_own(part, x_to, slot):
        ref, dst = query_refs[part]
        return remote(
            ref.at[:, :, head_lanes(parity, width)], dst.at[slot],
            q_ss.at[part, x_to], q_rs.at[part, slot], at_x(x_to),
        )

    def query_mate(part, x_to, slot):
        dst = query_refs[part][1]
        return remote(
            dst.at[mate], dst.at[slot],
            q_ss.at[part, xs + x_to], q_rs.at[part, slot], at_x(x_to),
        )

    for order in range(1, zs):
        key_z(z_of(order), z).start()
    for order in range(1, ys):
        value_y(y_of(order), y).start()
    for part in range(2):
        query_pair(part, me).start()
    for part in range(2):
        for hop in range(1, xs):
            query_own(part, lax.rem(x + hop, xs), me).start()
    own = [
        pltpu.make_async_copy(
            key_ref.at[:, :, head_lanes(parity, HD)], key_all.at[y, core, z], local_sem.at[0]
        ),
        pltpu.make_async_copy(value_ref, value_stage.at[y], local_sem.at[1]),
    ]
    own += [
        pltpu.make_async_copy(
            ref.at[:, :, head_lanes(parity, width)], dst.at[me], local_sem.at[2 + part]
        )
        for part, (ref, dst) in enumerate(query_refs)
    ]
    for copy in own:
        copy.start()

    row_of = lax.broadcasted_iota(jnp.int32, (ROWS, toks), 0)

    def fill_positions(y_at, carry):
        for core_at in range(2):
            for z_at in range(zs):
                for half in range(2):
                    block = ((y_at * zhs + z_at // zls) * 2 + core_at) * 2 + half
                    first = order_ref[block] * block_len + (x * zls + z_at % zls) * ROWS
                    group = (core_at * zs + z_at) * 2 + half
                    key_pos[y_at, group * ROWS:(group + 1) * ROWS, :] = row_of + first
        return carry

    lax.fori_loop(0, ys, fill_positions, 0)
    token = lax.broadcasted_iota(jnp.int32, (1, toks), 1)
    half_of = lax.rem(lax.div(token, ROWS), 2)
    pair_of = lax.rem(lax.div(token, 2 * ROWS), 2)
    x_of = lax.div(token, 4 * ROWS)
    block_pos = jnp.where(half_of == 0, order_ref[ctx * 2], order_ref[ctx * 2 + 1])
    query_pos = (
        block_pos * block_len
        + (x_of * zls + (zl - parity) + pair_of) * ROWS
        + lax.rem(token, ROWS)
    )
    attended_acc[...] = jnp.zeros_like(attended_acc)
    query_acc[...] = jnp.zeros_like(query_acc)

    def key_y(peer, slot):
        return remote(
            key_all.at[slot, core], key_all.at[slot, core],
            ky_ss.at[peer], ky_rs.at[slot], at_y(peer),
        )

    def value_z(peer, slot):
        return remote(
            value_stage.at[:, :, :, head_lanes(lax.rem(peer, 2), HD)],
            value_all.at[:, core, slot], vz_ss.at[peer], vz_rs.at[slot], at_z(peer),
        )

    def key_sibling(y_at, core_at):
        ref = key_all.at[y_at, core_at]
        return remote(ref, ref, sk_ss.at[y_at], sk_rs.at[y_at], sibling)

    def value_sibling(z_at, core_at):
        ref = value_all.at[:, core_at, z_at]
        return remote(ref, ref, sv_ss.at[z_at], sv_rs.at[z_at], sibling)

    for copy in own:
        copy.wait()
    for order in range(1, zs):
        key_z(z, z_of(order)).wait_recv()
    for order in range(1, ys):
        key_y(y_of(order), y).start()
    key_sibling(y, core).start()
    for order in range(1, ys):
        value_y(y, y_of(order)).wait_recv()
    for order in range(1, zs):
        value_z(z_of(order), z).start()
    own_value = pltpu.make_async_copy(
        value_stage.at[:, :, :, head_lanes(parity, HD)], value_all.at[:, core, z],
        local_sem.at[4],
    )
    own_value.start()
    for part in range(2):
        query_pair(part, mate).wait_recv()
        for hop in range(1, xs):
            query_mate(part, lax.rem(x + hop, xs), mate).start()
    own_value.wait()
    value_sibling(z, core).start()
    for part in range(2):
        for hop in range(1, xs):
            other = lax.rem(x + hop, xs)
            query_own(part, x, other * 2 + parity).wait_recv()
            query_mate(part, x, other * 2 + 1 - parity).wait_recv()
    for head_at in range(GROUP):
        lanes = slice(head_at * HD, (head_at + 1) * HD)
        rows = slice(head_at * toks, (head_at + 1) * toks)
        for src, by_row, by_col in (
            (query_all, query_rows, query_cols), (grad_all, grad_rows, grad_cols)
        ):
            tile = src[:, :, :, lanes].astype(F32).reshape(toks, HD)
            by_row[rows, :] = tile.astype(BF16)
            by_col[:, rows] = tile.T.astype(BF16)

    def pass_key(order):
        y_at = y_of(order)
        key_y(y, y_at).wait_recv()
        key_sibling(y_at, core).start()

    def pass_value(order):
        z_at = z_of(order)
        value_z(z, z_at).wait_recv()
        value_sibling(z_at, core).start()

    def score(order, carry):
        @pl.when(order + 1 < ys)
        def _():
            pass_key(order + 1)

        @pl.when(order + 1 < zs)
        def _():
            pass_value(order + 1)

        y_at = y_of(order)
        key_sibling(y_at, 1 - core).wait_recv()
        key_wide = key_all[y_at].astype(F32).reshape(keys, HD)
        key_cols[y_at] = key_wide.T.astype(BF16)
        key_tile = key_wide.astype(BF16)
        allowed = jnp.concatenate([key_pos[y_at]] * (step // toks), axis=1) <= jnp.concatenate(
            [query_pos] * (step // toks), axis=1
        )
        for first in range(0, cols, step):
            lanes = slice(first, first + step)
            scores = jnp.where(allowed, matmul(key_tile, query_cols[:, lanes]), LOWEST)
            top = jnp.max(scores, axis=0, keepdims=True)
            exp_tile = jnp.exp2((scores - top) * exp_scale)
            exps[y_at, :, lanes] = exp_tile
            max_rows[pl.ds(y_at, 1), lanes] = top
            sum_rows[pl.ds(y_at, 1), lanes] = jnp.sum(exp_tile, axis=0, keepdims=True)
        return carry

    lax.fori_loop(0, ys, score, 0)
    for order in range(ys + 1, zs):
        pass_value(order)
    for order in range(zs):
        value_sibling(z_of(order), 1 - core).wait_recv()

    def weigh(y_at, carry):
        value_wide = value_all[y_at].astype(F32).reshape(keys, HD)
        value_cols[y_at] = value_wide.T.astype(BF16)
        value_tile = value_wide.astype(BF16)
        for first in range(0, cols, step):
            lanes = slice(first, first + step)
            weight_grad = matmul(value_tile, grad_cols[:, lanes])
            grad_weights[y_at, :, lanes] = weight_grad
            dot_rows[pl.ds(y_at, 1), lanes] = jnp.sum(
                exps[y_at, :, lanes] * weight_grad, axis=0, keepdims=True
            )
        return carry

    lax.fori_loop(0, ys, weigh, 0)

    top = jnp.max(max_rows[...], axis=0, keepdims=True)
    factor = jnp.exp2((max_rows[...] - top) * exp_scale)
    ratio_rows[...] = factor
    scale_row[...] = top
    for index, row in enumerate((
        top,
        jnp.sum(sum_rows[...] * factor, axis=0, keepdims=True),
        jnp.sum(dot_rows[...] * factor, axis=0, keepdims=True),
    )):
        for head_at in range(GROUP):
            stat_all[x, index, head_at:head_at + 1, :] = row[
                :, head_at * toks:(head_at + 1) * toks
            ]

    def stat_copy(peer, slot):
        return remote(
            stat_all.at[slot], stat_all.at[slot], stat_ss.at[peer], stat_rs.at[slot], at_x(peer)
        )

    for hop in range(1, xs):
        stat_copy(lax.rem(x + hop, xs), x).start()

    for order in range(zs):
        peer = z_of(order)
        value_sibling(peer, core).wait_send()
        if order:
            key_z(peer, z).wait_send()
            value_z(peer, z).wait_send()
    for order in range(ys):
        peer = y_of(order)
        key_sibling(peer, core).wait_send()
        if order:
            value_y(peer, y).wait_send()
            key_y(peer, y).wait_send()
    for part in range(2):
        query_pair(part, me).wait_send()
        for hop in range(1, xs):
            query_own(part, lax.rem(x + hop, xs), me).wait_send()
            query_mate(part, lax.rem(x + hop, xs), mate).wait_send()

    def attend(y_at, carry):
        for first in range(0, cols, step):
            lanes = slice(first, first + step)
            weights = exps[y_at, :, lanes] * ratio_rows[pl.ds(y_at, 1), lanes]
            attended_acc[:, lanes] += matmul(value_cols[y_at], weights.astype(BF16))
        return carry

    lax.fori_loop(0, ys, attend, 0)

    for hop in range(1, xs):
        stat_copy(x, lax.rem(x + hop, xs)).wait_recv()
        stat_copy(lax.rem(x + hop, xs), x).wait_send()
    tops = [stat_all[x_at, 0] for x_at in range(xs)]
    top = functools.reduce(jnp.maximum, tops)
    factors = [jnp.exp2((part - top) * exp_scale) for part in tops]
    total = sum(stat_all[x_at, 1] * factors[x_at] for x_at in range(xs))
    inverse = 1.0 / total
    delta = sum(stat_all[x_at, 2] * factors[x_at] for x_at in range(xs)) * inverse
    for head_at in range(GROUP):
        lanes = slice(head_at * toks, (head_at + 1) * toks)
        row = slice(head_at, head_at + 1)
        delta_row[:, lanes] = delta[row]
        scale_row[:, lanes] = (
            jnp.exp2((scale_row[:, lanes] - top[row]) * exp_scale) * inverse[row]
        )
        ratio_rows[:, lanes] = (
            jnp.exp2((max_rows[:, lanes] - top[row]) * exp_scale) * inverse[row]
        )

    def out_x(part, peer, slot):
        return remote(
            out_part.at[part, peer], out_in.at[part, slot],
            ox_ss.at[part, peer], ox_rs.at[part, slot], at_x(peer),
        )

    def out_pair(part):
        return remote(
            pair_send.at[part], pair_in.at[part], oz_ss.at[part], oz_rs.at[part], mate_device
        )

    def send_out(part, acc, scale):
        for head_at in range(GROUP):
            lanes = slice(head_at * HD, (head_at + 1) * HD)
            rows = slice(head_at * toks, (head_at + 1) * toks)
            out_part[part, :, :, :, :, lanes] = (
                (acc[:, rows] * scale(rows)).T.reshape(xs, 2, 2, ROWS, HD).astype(BF16)
            )
        for hop in range(1, xs):
            out_x(part, lax.rem(x + hop, xs), x).start()
        out_in[part, x] = out_part[part, x]

    def add_out(part, out):
        for hop in range(1, xs):
            out_x(part, x, lax.rem(x + hop, xs)).wait_recv()
        pair_send[part] = sum(
            out_in[part, x_at, 1 - parity].astype(F32) for x_at in range(xs)
        ).astype(BF16)
        out_pair(part).start()
        out[:, :, head_lanes(parity, width)] = sum(
            out_in[part, x_at, parity].astype(F32) for x_at in range(xs)
        ).astype(BF16)

    send_out(0, attended_acc, lambda rows: scale_row[:, rows])

    def dsib_copy(order, core_at):
        return remote(
            kv_part.at[order, core_at], sibling_in.at[order],
            dsib_ss.at[order], dsib_rs.at[order], sibling,
        )

    def dkey_y(order):
        return remote(
            key_send.at[order], key_in.at[order],
            dky_ss.at[order], dky_rs.at[order], at_y(y_of(order)),
        )

    def dvalue_z(order, peer, slot):
        return remote(
            value_send.at[peer, order], value_in.at[slot, order],
            dvz_ss.at[peer], dvz_rs.at[slot], at_z(peer),
        )

    def dvalue_all(peer, slot):
        return remote(
            value_send.at[peer], value_in.at[slot], dvz_ss.at[peer], dvz_rs.at[slot], at_z(peer)
        )

    def add_sibling(order):
        dsib_copy(order, 1 - core).wait_recv()
        key_send[order] = (
            kv_part[order, core, 0].astype(F32) + sibling_in[order, 0].astype(F32)
        ).astype(BF16)
        value_send[:, order] = (
            kv_part[order, core, 1].astype(F32) + sibling_in[order, 1].astype(F32)
        ).astype(BF16)
        for near in range(1, zs):
            dvalue_z(order, z_of(near), z).start()

    def backward(turn, carry):
        order = ys - 1 - turn
        y_at = y_of(order)
        key_sum = jnp.zeros((keys, HD), F32)
        value_sum = jnp.zeros((keys, HD), F32)
        for first in range(0, cols, step):
            lanes = slice(first, first + step)
            probs = exps[y_at, :, lanes] * ratio_rows[pl.ds(y_at, 1), lanes]
            weights = probs.astype(BF16)
            grad_scores = (
                probs * (grad_weights[y_at, :, lanes] - delta_row[:, lanes])
            ).astype(BF16)
            query_acc[:, lanes] += matmul(key_cols[y_at], grad_scores)
            value_sum += matmul(weights, grad_rows[lanes, :])
            key_sum += matmul(grad_scores, query_rows[lanes, :])
        shape = (2, zs, 2, ROWS, HD)
        kv_part[order, :, 0] = (key_sum * scaling).reshape(shape).astype(BF16)
        kv_part[order, :, 1] = value_sum.reshape(shape).astype(BF16)
        dsib_copy(order, 1 - core).start()

        @pl.when(turn >= 1)
        def _():
            add_sibling(order + 1)
            dkey_y(order + 1).start()

        return carry

    lax.fori_loop(0, ys, backward, 0)

    send_out(1, query_acc, lambda rows: scaling)
    add_out(0, attended_out)
    add_sibling(0)
    value_in[z] = value_send[z]

    total_key = key_send[0].astype(F32)
    for order in range(1, ys):
        dkey_y(order).wait_recv()
        total_key += key_in[order].astype(F32)
    key_last[...] = total_key.astype(BF16)

    def dkey_z(peer, slot):
        return remote(
            key_last.at[peer], key_home.at[slot], dkz_ss.at[peer], dkz_rs.at[slot], at_z(peer)
        )

    def dvalue_y(order):
        return remote(
            value_last.at[order], value_home.at[order],
            dvy_ss.at[order], dvy_rs.at[order], at_y(y_of(order)),
        )

    for near in range(1, zs):
        dkey_z(z_of(near), z).start()
    key_home[z] = key_last[z]
    for near in range(1, zs):
        dvalue_all(z, z_of(near)).wait_recv()
    for half in range(2):
        value_last[:, half] = sum(
            value_in[z_at].astype(F32) for z_at in range(half, zs, 2)
        ).astype(BF16)
    for order in range(1, ys):
        dvalue_y(order).start()
    value_home[0] = value_last[0]

    add_out(1, query_out)
    for near in range(1, zs):
        dkey_z(z, z_of(near)).wait_recv()
    for half in range(2):
        key_out[:, :, half * HD:(half + 1) * HD] = sum(
            key_home[z_at].astype(F32) for z_at in range(half, zs, 2)
        ).astype(BF16)
    for order in range(1, ys):
        dvalue_y(order).wait_recv()
    for half in range(2):
        value_out[:, :, half * HD:(half + 1) * HD] = sum(
            value_home[order, half].astype(F32) for order in range(ys)
        ).astype(BF16)
    for part, out in enumerate((attended_out, query_out)):
        out_pair(part).wait_recv()
        out[:, :, head_lanes(1 - parity, width)] = pair_in[part]

    for order in range(1, zs):
        peer = z_of(order)
        dkey_z(peer, z).wait_send()
        dvalue_all(peer, z).wait_send()
    for order in range(ys):
        dsib_copy(order, 1 - core).wait_send()
        if order:
            dkey_y(order).wait_send()
            dvalue_y(order).wait_send()
    for part in range(2):
        for hop in range(1, xs):
            out_x(part, lax.rem(x + hop, xs), x).wait_send()
        out_pair(part).wait_send()


def finish(*refs):
    for src, dst in zip(refs[:4], refs[4:]):
        dst[...] = src[...]


def shards(split, queries, key_vectors, value_vectors, out_grad, block_order):
    xs, zls, ys, zhs = split["x"], split["z_lo"], split["y"], split["z_hi"]
    zs, srcs = zls * zhs, 2 * xs
    toks = srcs * 2 * ROWS
    cols = GROUP * toks
    keys = 2 * zs * 2 * ROWS
    width = GROUP * HD
    vmem = pltpu.VMEM
    dma = pltpu.SemaphoreType.DMA
    tile = (2, ROWS, HD)
    whole = pl.BlockSpec(memory_space=pltpu.VMEM)
    results = tuple(
        jax.ShapeDtypeStruct(a.shape, BF16)
        for a in (queries, queries, key_vectors, value_vectors)
    )
    partial_sums = pl.pallas_call(
        functools.partial(kernel, split),
        out_shape=results,
        in_specs=[pl.BlockSpec(memory_space=pl.ANY)] * 4
        + [pl.BlockSpec(memory_space=pltpu.SMEM)],
        out_specs=(whole,) * 4,
        scratch_shapes=[
            vmem((srcs, 2, ROWS, width), BF16), vmem((srcs, 2, ROWS, width), BF16),
            vmem((ys, 2, zs) + tile, BF16), vmem((ys, 2, zs) + tile, BF16),
            vmem((ys,) + value_vectors.shape, BF16),
            vmem((cols, HD), BF16), vmem((cols, HD), BF16),
            vmem((HD, cols), BF16), vmem((HD, cols), BF16),
            vmem((ys, HD, keys), BF16), vmem((ys, HD, keys), BF16),
            vmem((ys, keys, toks), jnp.int32),
            vmem((ys, keys, cols), F32), vmem((ys, keys, cols), F32),
            vmem((ys, cols), F32), vmem((ys, cols), F32), vmem((ys, cols), F32),
            vmem((ys, cols), F32), vmem((1, cols), F32), vmem((1, cols), F32),
            vmem((xs, 3, GROUP, toks), F32),
            vmem((HD, cols), F32), vmem((HD, cols), F32),
            vmem((2, xs, 2, 2, ROWS, width), BF16), vmem((2, xs, 2, 2, ROWS, width), BF16),
            vmem((2, 2, ROWS, width), BF16), vmem((2, 2, ROWS, width), BF16),
            vmem((ys, 2, 2, zs) + tile, BF16), vmem((ys, 2, zs) + tile, BF16),
            vmem((ys, zs) + tile, BF16), vmem((ys, zs) + tile, BF16),
            vmem((zs, ys) + tile, BF16), vmem((zs, ys) + tile, BF16),
            vmem((zs,) + tile, BF16), vmem((zs,) + tile, BF16),
            vmem((ys, 2) + tile, BF16), vmem((ys, 2) + tile, BF16),
            dma((2, 2 * xs)), dma((2, srcs)), dma((zs,)), dma((zs,)), dma((ys,)), dma((ys,)),
            dma((ys,)), dma((ys,)), dma((zs,)), dma((zs,)),
            dma((ys,)), dma((ys,)), dma((zs,)), dma((zs,)), dma((xs,)), dma((xs,)),
            dma((ys,)), dma((ys,)),
            dma((ys,)), dma((ys,)), dma((zs,)), dma((zs,)),
            dma((zs,)), dma((zs,)), dma((ys,)), dma((ys,)),
            dma((2, xs)), dma((2, xs)), dma((2,)), dma((2,)), dma((5,)),
        ],
        compiler_params=pltpu.CompilerParams(
            collective_id=0, has_side_effects=True, vmem_limit_bytes=56 * 1024 * 1024
        ),
        name="attention",
    )(queries, out_grad, key_vectors, value_vectors, block_order)
    return pl.pallas_call(
        finish, out_shape=results, in_specs=[whole] * 4, out_specs=(whole,) * 4, name="finish"
    )(*partial_sums)


def solution(mesh, split=SPLIT):
    rows = P("ctx", "head", None)
    return jax.shard_map(
        functools.partial(shards, split),
        mesh=mesh,
        in_specs=(rows, rows, rows, rows, P()),
        out_specs=(rows,) * 4,
        check_vma=False,
    )
```

```python
import functools
import math

import jax
import jax.numpy as jnp
from jax import lax
from jax.experimental import pallas as pl
from jax.experimental.pallas import tpu as pltpu
from jax.sharding import PartitionSpec as P

HD = 128
GROUP = 8
ROWS = 8
LOWEST = -1e30
MESH = pl.DeviceIdType.MESH
F32 = jnp.float32
BF16 = jnp.bfloat16

AHEAD = 2

SPLIT = dict(x=4, z_lo=4, y=8, z_hi=2)


def matmul(left_side, right_side):
    return lax.dot_general(
        left_side, right_side, (((1,), (0,)), ((), ())), preferred_element_type=F32
    )


def kernel(
    split,
    query_ref, grad_ref, key_ref, value_ref, order_ref,
    attended_out, query_out, key_out, value_out,
    query_all, grad_all, key_all, value_all, value_stage,
    query_rows, grad_rows, query_cols, grad_cols, key_cols,
    key_pos, exps, exps_low, grad_weights,
    max_rows, sum_rows, ratio_rows, delta_row, scale_row, stat_all,
    attended_acc, query_acc, out_part, out_in, pair_send, pair_in,
    kv_part, sibling_in, key_send, key_in, value_send, value_in,
    key_last, key_home, value_last, value_home,
    q_ss, q_rs, kz_ss, kz_rs, ky_ss, ky_rs, vy_ss, vy_rs, vz_ss, vz_rs,
    sk_ss, sk_rs, sv_ss, sv_rs, stat_ss, stat_rs, dsib_ss, dsib_rs,
    dky_ss, dky_rs, dkz_ss, dkz_rs, dvz_ss, dvz_rs, dvy_ss, dvy_rs,
    ox_ss, ox_rs, oz_ss, oz_rs, local_sem,
):
    xs, zls, ys, zhs = split["x"], split["z_lo"], split["y"], split["z_hi"]
    zs, srcs = zls * zhs, 2 * xs
    toks = srcs * 2 * ROWS
    cols = GROUP * toks
    keys = 2 * zs * 2 * ROWS
    width = GROUP * HD
    block_len = xs * zls * ROWS
    step = min(256, cols)
    scaling = 1.0 / math.sqrt(HD)
    exp_scale = scaling / math.log(2.0)

    head, ctx = lax.axis_index("head"), lax.axis_index("ctx")
    x, zl = lax.div(head, zls), lax.rem(head, zls)
    core = lax.rem(ctx, 2)
    zh = lax.rem(lax.div(ctx, 2), zhs)
    y = lax.div(ctx, 2 * zhs)
    z = zh * zls + zl
    parity = lax.rem(zl, 2)
    me, mate = x * 2 + parity, x * 2 + 1 - parity

    def at(x_to, y_to, z_to, core_to):
        zh_to, zl_to = lax.div(z_to, zls), lax.rem(z_to, zls)
        return {"head": x_to * zls + zl_to, "ctx": (y_to * zhs + zh_to) * 2 + core_to}

    def at_x(x_to):
        return at(x_to, y, z, core)

    def at_y(y_to):
        return at(x, y_to, z, core)

    def at_z(z_to):
        return at(x, y, z_to, core)

    sibling = at(x, y, z, 1 - core)
    mate_device = at_z(z + 1 - 2 * parity)

    def remote(src, dst, send, recv, device):
        return pltpu.make_async_remote_copy(
            src_ref=src, dst_ref=dst, send_sem=send, recv_sem=recv,
            device_id=device, device_id_type=MESH,
        )

    def nearest(own, order, size):
        odd = lax.rem(order, 2)
        return lax.rem(
            own + odd * (size - lax.div(order + 1, 2)) + (1 - odd) * lax.div(order, 2), size
        )

    def y_of(order):
        return nearest(y, order, ys)

    def z_of(order):
        return nearest(z, order, zs)

    def head_lanes(index, size):
        return pl.ds(pl.multiple_of(index * size, HD), size)

    barrier = pltpu.get_barrier_semaphore()
    greeted = [sibling]
    greeted += [at_x(lax.rem(x + hop, xs)) for hop in range(1, xs)]
    greeted += [at_y(lax.rem(y + hop, ys)) for hop in range(1, ys)]
    greeted += [at_z(lax.rem(z + hop, zs)) for hop in range(1, zs)]
    for device in greeted:
        pl.semaphore_signal(barrier, inc=1, device_id=device, device_id_type=MESH)
    pl.semaphore_wait(barrier, len(greeted))

    def key_z(peer, slot):
        return remote(
            key_ref.at[:, :, head_lanes(lax.rem(peer, 2), HD)], key_all.at[y, core, slot],
            kz_ss.at[peer], kz_rs.at[slot], at_z(peer),
        )

    def value_y(peer, slot):
        return remote(
            value_ref, value_stage.at[slot], vy_ss.at[peer], vy_rs.at[slot], at_y(peer)
        )

    query_refs = ((query_ref, query_all), (grad_ref, grad_all))

    def query_pair(part, slot):
        ref, dst = query_refs[part]
        return remote(
            ref.at[:, :, head_lanes(1 - parity, width)], dst.at[slot],
            q_ss.at[part, x], q_rs.at[part, slot], mate_device,
        )

    def query_own(part, x_to, slot):
        ref, dst = query_refs[part]
        return remote(
            ref.at[:, :, head_lanes(parity, width)], dst.at[slot],
            q_ss.at[part, x_to], q_rs.at[part, slot], at_x(x_to),
        )

    def query_mate(part, x_to, slot):
        dst = query_refs[part][1]
        return remote(
            dst.at[mate], dst.at[slot],
            q_ss.at[part, xs + x_to], q_rs.at[part, slot], at_x(x_to),
        )

    for order in reversed(range(1, zs)):
        key_z(z_of(order), z).start()
    for order in reversed(range(1, ys)):
        value_y(y_of(order), y).start()
    for part in range(2):
        query_pair(part, me).start()
    for part in range(2):
        for hop in range(1, xs):
            query_own(part, lax.rem(x + hop, xs), me).start()
    own = [
        pltpu.make_async_copy(
            key_ref.at[:, :, head_lanes(parity, HD)], key_all.at[y, core, z], local_sem.at[0]
        ),
        pltpu.make_async_copy(value_ref, value_stage.at[y], local_sem.at[1]),
    ]
    own += [
        pltpu.make_async_copy(
            ref.at[:, :, head_lanes(parity, width)], dst.at[me], local_sem.at[2 + part]
        )
        for part, (ref, dst) in enumerate(query_refs)
    ]
    for copy in own:
        copy.start()

    row_of = lax.broadcasted_iota(jnp.int32, (ROWS, toks), 0)

    def fill_positions(y_at, carry):
        for core_at in range(2):
            for z_at in range(zs):
                for half in range(2):
                    block = ((y_at * zhs + z_at // zls) * 2 + core_at) * 2 + half
                    first = order_ref[block] * block_len + (x * zls + z_at % zls) * ROWS
                    group = (core_at * zs + z_at) * 2 + half
                    key_pos[y_at, group * ROWS:(group + 1) * ROWS, :] = row_of + first
        return carry

    lax.fori_loop(0, ys, fill_positions, 0)
    token = lax.broadcasted_iota(jnp.int32, (1, toks), 1)
    half_of = lax.rem(lax.div(token, ROWS), 2)
    pair_of = lax.rem(lax.div(token, 2 * ROWS), 2)
    x_of = lax.div(token, 4 * ROWS)
    block_pos = jnp.where(half_of == 0, order_ref[ctx * 2], order_ref[ctx * 2 + 1])
    query_pos = (
        block_pos * block_len
        + (x_of * zls + (zl - parity) + pair_of) * ROWS
        + lax.rem(token, ROWS)
    )
    attended_acc[...] = jnp.zeros_like(attended_acc)
    query_acc[...] = jnp.zeros_like(query_acc)

    def key_y(peer, slot):
        return remote(
            key_all.at[slot, core], key_all.at[slot, core],
            ky_ss.at[peer], ky_rs.at[slot], at_y(peer),
        )

    def value_z(peer, slot):
        return remote(
            value_stage.at[:, :, :, head_lanes(lax.rem(peer, 2), HD)],
            value_all.at[:, core, slot], vz_ss.at[peer], vz_rs.at[slot], at_z(peer),
        )

    def key_sibling(y_at, core_at):
        ref = key_all.at[y_at, core_at]
        return remote(ref, ref, sk_ss.at[y_at], sk_rs.at[y_at], sibling)

    def value_sibling(z_at, core_at):
        ref = value_all.at[:, core_at, z_at]
        return remote(ref, ref, sv_ss.at[z_at], sv_rs.at[z_at], sibling)

    for copy in own:
        copy.wait()
    for order in range(1, zs):
        key_z(z, z_of(order)).wait_recv()
    for order in range(1, ys):
        key_y(y_of(order), y).start()
    key_sibling(y, core).start()
    for order in range(1, ys):
        value_y(y, y_of(order)).wait_recv()
    for order in range(1, zs):
        value_z(z_of(order), z).start()
    own_value = pltpu.make_async_copy(
        value_stage.at[:, :, :, head_lanes(parity, HD)], value_all.at[:, core, z],
        local_sem.at[4],
    )
    own_value.start()
    for part in range(2):
        query_pair(part, mate).wait_recv()
        for hop in range(1, xs):
            query_mate(part, lax.rem(x + hop, xs), mate).start()
    own_value.wait()
    value_sibling(z, core).start()
    for part in range(2):
        for hop in range(1, xs):
            other = lax.rem(x + hop, xs)
            query_own(part, x, other * 2 + parity).wait_recv()
            query_mate(part, x, other * 2 + 1 - parity).wait_recv()
    for head_at in range(GROUP):
        lanes = slice(head_at * HD, (head_at + 1) * HD)
        rows = slice(head_at * toks, (head_at + 1) * toks)
        for src, by_row, by_col in (
            (query_all, query_rows, query_cols), (grad_all, grad_rows, grad_cols)
        ):
            tile = src[:, :, :, lanes].astype(F32).reshape(toks, HD)
            by_row[rows, :] = tile.astype(BF16)
            by_col[:, rows] = tile.T.astype(BF16)

    def pass_key(order):
        y_at = y_of(order)
        key_y(y, y_at).wait_recv()
        key_sibling(y_at, core).start()

    def pass_value(order):
        z_at = z_of(order)
        value_z(z, z_at).wait_recv()
        value_sibling(z_at, core).start()

    def score(order, carry):
        @pl.when(order + AHEAD < ys)
        def _():
            pass_key(order + AHEAD)

        @pl.when(order + AHEAD < zs)
        def _():
            pass_value(order + AHEAD)

        y_at = y_of(order)
        key_sibling(y_at, 1 - core).wait_recv()
        key_wide = key_all[y_at].astype(F32).reshape(keys, HD)
        key_cols[y_at] = key_wide.T.astype(BF16)
        key_tile = key_wide.astype(BF16)
        allowed = jnp.concatenate([key_pos[y_at]] * (step // toks), axis=1) <= jnp.concatenate(
            [query_pos] * (step // toks), axis=1
        )
        for first in range(0, cols, step):
            lanes = slice(first, first + step)
            scores = jnp.where(allowed, matmul(key_tile, query_cols[:, lanes]), LOWEST)
            top = jnp.max(scores, axis=0, keepdims=True)
            exp_tile = jnp.exp2((scores - top) * exp_scale)
            exps[y_at, :, lanes] = exp_tile
            exps_low[y_at, :, lanes] = exp_tile.astype(BF16)
            max_rows[pl.ds(y_at, 1), lanes] = top
            sum_rows[pl.ds(y_at, 1), lanes] = jnp.sum(exp_tile, axis=0, keepdims=True)
        return carry

    for order in range(1, AHEAD):
        pass_key(jnp.int32(order))
        pass_value(jnp.int32(order))
    lax.fori_loop(0, ys, score, 0)
    for order in range(ys + AHEAD, zs):
        pass_value(order)
    top = jnp.max(max_rows[...], axis=0, keepdims=True)
    factor = jnp.exp2((max_rows[...] - top) * exp_scale)
    ratio_rows[...] = factor
    scale_row[...] = top
    total = jnp.sum(sum_rows[...] * factor, axis=0, keepdims=True)
    for order in range(zs):
        value_sibling(z_of(order), 1 - core).wait_recv()

    def attend(y_at, carry):
        value_cols = value_all[y_at].astype(F32).reshape(keys, HD).T.astype(BF16)
        for first in range(0, cols, step):
            lanes = slice(first, first + step)
            attended_acc[:, lanes] += (
                matmul(value_cols, exps_low[y_at, :, lanes]) * ratio_rows[pl.ds(y_at, 1), lanes]
            )
        return carry

    lax.fori_loop(0, ys, attend, 0)

    dots = jnp.sum(attended_acc[...] * grad_cols[...].astype(F32), axis=0, keepdims=True)
    for index, row in enumerate((top, total, dots)):
        for head_at in range(GROUP):
            stat_all[x, index, head_at:head_at + 1, :] = row[
                :, head_at * toks:(head_at + 1) * toks
            ]

    def stat_copy(peer, slot):
        return remote(
            stat_all.at[slot], stat_all.at[slot], stat_ss.at[peer], stat_rs.at[slot], at_x(peer)
        )

    for hop in range(1, xs):
        stat_copy(lax.rem(x + hop, xs), x).start()

    for order in range(zs):
        peer = z_of(order)
        value_sibling(peer, core).wait_send()
        if order:
            key_z(peer, z).wait_send()
            value_z(peer, z).wait_send()
    for order in range(ys):
        peer = y_of(order)
        key_sibling(peer, core).wait_send()
        if order:
            value_y(peer, y).wait_send()
            key_y(peer, y).wait_send()
    for part in range(2):
        query_pair(part, me).wait_send()
        for hop in range(1, xs):
            query_own(part, lax.rem(x + hop, xs), me).wait_send()
            query_mate(part, lax.rem(x + hop, xs), mate).wait_send()

    def weigh(y_at, carry):
        value_tile = value_all[y_at].astype(F32).reshape(keys, HD).astype(BF16)
        for first in range(0, cols, step):
            lanes = slice(first, first + step)
            grad_weights[y_at, :, lanes] = matmul(value_tile, grad_cols[:, lanes])
        return carry

    lax.fori_loop(0, ys, weigh, 0)

    for hop in range(1, xs):
        stat_copy(x, lax.rem(x + hop, xs)).wait_recv()
        stat_copy(lax.rem(x + hop, xs), x).wait_send()
    tops = [stat_all[x_at, 0] for x_at in range(xs)]
    top = functools.reduce(jnp.maximum, tops)
    factors = [jnp.exp2((part - top) * exp_scale) for part in tops]
    total = sum(stat_all[x_at, 1] * factors[x_at] for x_at in range(xs))
    inverse = 1.0 / total
    delta = sum(stat_all[x_at, 2] * factors[x_at] for x_at in range(xs)) * inverse
    for head_at in range(GROUP):
        lanes = slice(head_at * toks, (head_at + 1) * toks)
        row = slice(head_at, head_at + 1)
        delta_row[:, lanes] = delta[row]
        scale_row[:, lanes] = (
            jnp.exp2((scale_row[:, lanes] - top[row]) * exp_scale) * inverse[row]
        )
        ratio_rows[:, lanes] = (
            jnp.exp2((max_rows[:, lanes] - top[row]) * exp_scale) * inverse[row]
        )

    def out_x(part, peer, slot):
        return remote(
            out_part.at[part, peer], out_in.at[part, slot],
            ox_ss.at[part, peer], ox_rs.at[part, slot], at_x(peer),
        )

    def out_pair(part):
        return remote(
            pair_send.at[part], pair_in.at[part], oz_ss.at[part], oz_rs.at[part], mate_device
        )

    def send_out(part, acc, scale):
        for head_at in range(GROUP):
            lanes = slice(head_at * HD, (head_at + 1) * HD)
            rows = slice(head_at * toks, (head_at + 1) * toks)
            out_part[part, :, :, :, :, lanes] = (
                (acc[:, rows] * scale(rows)).T.reshape(xs, 2, 2, ROWS, HD).astype(BF16)
            )
        for hop in range(1, xs):
            out_x(part, lax.rem(x + hop, xs), x).start()
        out_in[part, x] = out_part[part, x]

    def add_out(part, out):
        for hop in range(1, xs):
            out_x(part, x, lax.rem(x + hop, xs)).wait_recv()
        pair_send[part] = sum(
            out_in[part, x_at, 1 - parity].astype(F32) for x_at in range(xs)
        ).astype(BF16)
        out_pair(part).start()
        out[:, :, head_lanes(parity, width)] = sum(
            out_in[part, x_at, parity].astype(F32) for x_at in range(xs)
        ).astype(BF16)

    send_out(0, attended_acc, lambda rows: scale_row[:, rows])

    def dsib_copy(order, core_at):
        return remote(
            kv_part.at[order, core_at], sibling_in.at[order],
            dsib_ss.at[order], dsib_rs.at[order], sibling,
        )

    def dkey_y(order):
        return remote(
            key_send.at[order], key_in.at[order],
            dky_ss.at[order], dky_rs.at[order], at_y(y_of(order)),
        )

    def dvalue_z(order, peer, slot):
        return remote(
            value_send.at[peer, order], value_in.at[slot, order],
            dvz_ss.at[peer], dvz_rs.at[slot], at_z(peer),
        )

    def dvalue_all(peer, slot):
        return remote(
            value_send.at[peer], value_in.at[slot], dvz_ss.at[peer], dvz_rs.at[slot], at_z(peer)
        )

    def add_sibling(order):
        dsib_copy(order, 1 - core).wait_recv()
        key_send[order] = (
            kv_part[order, core, 0].astype(F32) + sibling_in[order, 0].astype(F32)
        ).astype(BF16)
        value_send[:, order] = (
            kv_part[order, core, 1].astype(F32) + sibling_in[order, 1].astype(F32)
        ).astype(BF16)
        for near in reversed(range(1, zs)):
            dvalue_z(order, z_of(near), z).start()

    def backward(turn, carry):
        order = ys - 1 - turn
        y_at = y_of(order)
        key_sum = jnp.zeros((keys, HD), F32)
        value_sum = jnp.zeros((keys, HD), F32)
        for first in range(0, cols, step):
            lanes = slice(first, first + step)
            probs = exps[y_at, :, lanes] * ratio_rows[pl.ds(y_at, 1), lanes]
            weights = probs.astype(BF16)
            grad_scores = (
                probs * (grad_weights[y_at, :, lanes] - delta_row[:, lanes])
            ).astype(BF16)
            query_acc[:, lanes] += matmul(key_cols[y_at], grad_scores)
            value_sum += matmul(weights, grad_rows[lanes, :])
            key_sum += matmul(grad_scores, query_rows[lanes, :])
        shape = (2, zs, 2, ROWS, HD)
        kv_part[order, :, 0] = (key_sum * scaling).reshape(shape).astype(BF16)
        kv_part[order, :, 1] = value_sum.reshape(shape).astype(BF16)
        dsib_copy(order, 1 - core).start()

        @pl.when(turn >= 1)
        def _():
            add_sibling(order + 1)
            dkey_y(order + 1).start()

        return carry

    lax.fori_loop(0, ys, backward, 0)

    send_out(1, query_acc, lambda rows: scaling)
    add_out(0, attended_out)
    add_sibling(0)
    value_in[z] = value_send[z]

    total_key = key_send[0].astype(F32)
    for order in range(1, ys):
        dkey_y(order).wait_recv()
        total_key += key_in[order].astype(F32)
    key_last[...] = total_key.astype(BF16)

    def dkey_z(peer, slot):
        return remote(
            key_last.at[peer], key_home.at[slot], dkz_ss.at[peer], dkz_rs.at[slot], at_z(peer)
        )

    def dvalue_y(order):
        return remote(
            value_last.at[order], value_home.at[order],
            dvy_ss.at[order], dvy_rs.at[order], at_y(y_of(order)),
        )

    for near in reversed(range(1, zs)):
        dkey_z(z_of(near), z).start()
    key_home[z] = key_last[z]
    for near in range(1, zs):
        dvalue_all(z, z_of(near)).wait_recv()
    for half in range(2):
        value_last[:, half] = sum(
            value_in[z_at].astype(F32) for z_at in range(half, zs, 2)
        ).astype(BF16)
    for order in reversed(range(1, ys)):
        dvalue_y(order).start()
    value_home[0] = value_last[0]

    for order in range(ys):
        dsib_copy(order, 1 - core).wait_send()
        if order:
            dkey_y(order).wait_send()
    for order in range(1, zs):
        dvalue_all(z_of(order), z).wait_send()
    add_out(1, query_out)
    for part in range(2):
        for hop in range(1, xs):
            out_x(part, lax.rem(x + hop, xs), x).wait_send()
    for near in range(1, zs):
        dkey_z(z, z_of(near)).wait_recv()
    for half in range(2):
        key_out[:, :, half * HD:(half + 1) * HD] = sum(
            key_home[z_at].astype(F32) for z_at in range(half, zs, 2)
        ).astype(BF16)
    for order in range(1, ys):
        dvalue_y(order).wait_recv()
    for half in range(2):
        value_out[:, :, half * HD:(half + 1) * HD] = sum(
            value_home[order, half].astype(F32) for order in range(ys)
        ).astype(BF16)
    for part, out in enumerate((attended_out, query_out)):
        out_pair(part).wait_recv()
        out[:, :, head_lanes(1 - parity, width)] = pair_in[part]

    for order in range(1, zs):
        dkey_z(z_of(order), z).wait_send()
    for order in range(1, ys):
        dvalue_y(order).wait_send()
    for part in range(2):
        out_pair(part).wait_send()


def finish(*refs):
    for src, dst in zip(refs[:4], refs[4:]):
        dst[...] = src[...]


def shards(split, queries, key_vectors, value_vectors, out_grad, block_order):
    xs, zls, ys, zhs = split["x"], split["z_lo"], split["y"], split["z_hi"]
    zs, srcs = zls * zhs, 2 * xs
    toks = srcs * 2 * ROWS
    cols = GROUP * toks
    keys = 2 * zs * 2 * ROWS
    width = GROUP * HD
    vmem = pltpu.VMEM
    dma = pltpu.SemaphoreType.DMA
    tile = (2, ROWS, HD)
    whole = pl.BlockSpec(memory_space=pltpu.VMEM)
    results = tuple(
        jax.ShapeDtypeStruct(a.shape, BF16)
        for a in (queries, queries, key_vectors, value_vectors)
    )
    partial_sums = pl.pallas_call(
        functools.partial(kernel, split),
        out_shape=results,
        in_specs=[pl.BlockSpec(memory_space=pl.ANY)] * 4
        + [pl.BlockSpec(memory_space=pltpu.SMEM)],
        out_specs=(whole,) * 4,
        scratch_shapes=[
            vmem((srcs, 2, ROWS, width), BF16), vmem((srcs, 2, ROWS, width), BF16),
            vmem((ys, 2, zs) + tile, BF16), vmem((ys, 2, zs) + tile, BF16),
            vmem((ys,) + value_vectors.shape, BF16),
            vmem((cols, HD), BF16), vmem((cols, HD), BF16),
            vmem((HD, cols), BF16), vmem((HD, cols), BF16),
            vmem((ys, HD, keys), BF16),
            vmem((ys, keys, toks), jnp.int32),
            vmem((ys, keys, cols), F32), vmem((ys, keys, cols), BF16),
            vmem((ys, keys, cols), F32),
            vmem((ys, cols), F32), vmem((ys, cols), F32), vmem((ys, cols), F32), vmem((1, cols), F32), vmem((1, cols), F32),
            vmem((xs, 3, GROUP, toks), F32),
            vmem((HD, cols), F32), vmem((HD, cols), F32),
            vmem((2, xs, 2, 2, ROWS, width), BF16), vmem((2, xs, 2, 2, ROWS, width), BF16),
            vmem((2, 2, ROWS, width), BF16), vmem((2, 2, ROWS, width), BF16),
            vmem((ys, 2, 2, zs) + tile, BF16), vmem((ys, 2, zs) + tile, BF16),
            vmem((ys, zs) + tile, BF16), vmem((ys, zs) + tile, BF16),
            vmem((zs, ys) + tile, BF16), vmem((zs, ys) + tile, BF16),
            vmem((zs,) + tile, BF16), vmem((zs,) + tile, BF16),
            vmem((ys, 2) + tile, BF16), vmem((ys, 2) + tile, BF16),
            dma((2, 2 * xs)), dma((2, srcs)), dma((zs,)), dma((zs,)), dma((ys,)), dma((ys,)),
            dma((ys,)), dma((ys,)), dma((zs,)), dma((zs,)),
            dma((ys,)), dma((ys,)), dma((zs,)), dma((zs,)), dma((xs,)), dma((xs,)),
            dma((ys,)), dma((ys,)),
            dma((ys,)), dma((ys,)), dma((zs,)), dma((zs,)),
            dma((zs,)), dma((zs,)), dma((ys,)), dma((ys,)),
            dma((2, xs)), dma((2, xs)), dma((2,)), dma((2,)), dma((5,)),
        ],
        compiler_params=pltpu.CompilerParams(
            collective_id=0, has_side_effects=True, vmem_limit_bytes=56 * 1024 * 1024
        ),
        name="attention",
    )(queries, out_grad, key_vectors, value_vectors, block_order)
    return pl.pallas_call(
        finish, out_shape=results, in_specs=[whole] * 4, out_specs=(whole,) * 4, name="finish"
    )(*partial_sums)


def solution(mesh, split=SPLIT):
    rows = P("ctx", "head", None)
    return jax.shard_map(
        functools.partial(shards, split),
        mesh=mesh,
        in_specs=(rows, rows, rows, rows, P()),
        out_specs=(rows,) * 4,
        check_vma=False,
    )
```

```python
import functools
import math

import jax
import jax.numpy as jnp
from jax import lax
from jax.experimental import pallas as pl
from jax.experimental.pallas import tpu as pltpu
from jax.sharding import PartitionSpec as P

HD = 128
GROUP = 8
ROWS = 8
LOWEST = -1e30
MESH = pl.DeviceIdType.MESH
F32 = jnp.float32
BF16 = jnp.bfloat16

AHEAD = 2

SPLIT = dict(x=4, z_lo=4, y=8, z_hi=2)


def matmul(left_side, right_side):
    return lax.dot_general(
        left_side, right_side, (((1,), (0,)), ((), ())), preferred_element_type=F32
    )


def kernel(
    split,
    query_ref, grad_ref, key_ref, value_ref, order_ref,
    attended_out, query_out, key_out, value_out,
    query_all, grad_all, key_all, value_all, value_stage,
    query_rows, grad_rows, query_cols, grad_cols, key_cols,
    key_pos, exps, exps_low, grad_weights,
    max_rows, sum_rows, ratio_rows, delta_row, scale_row, stat_all,
    attended_acc, query_acc, out_part, out_in, pair_send, pair_in,
    kv_part, sibling_in, key_send, key_in, value_send, value_in,
    key_last, key_home, value_last, value_home,
    q_ss, q_rs, kz_ss, kz_rs, ky_ss, ky_rs, vy_ss, vy_rs, vz_ss, vz_rs,
    sk_ss, sk_rs, sv_ss, sv_rs, stat_ss, stat_rs, dsib_ss, dsib_rs,
    dky_ss, dky_rs, dkz_ss, dkz_rs, dvz_ss, dvz_rs, dvy_ss, dvy_rs,
    ox_ss, ox_rs, oz_ss, oz_rs, local_sem,
):
    xs, zls, ys, zhs = split["x"], split["z_lo"], split["y"], split["z_hi"]
    zs, srcs = zls * zhs, 2 * xs
    toks = srcs * 2 * ROWS
    cols = GROUP * toks
    keys = 2 * zs * 2 * ROWS
    width = GROUP * HD
    block_len = xs * zls * ROWS
    step = min(256, cols)
    scaling = 1.0 / math.sqrt(HD)
    exp_scale = scaling / math.log(2.0)

    head, ctx = lax.axis_index("head"), lax.axis_index("ctx")
    x, zl = lax.div(head, zls), lax.rem(head, zls)
    core = lax.rem(ctx, 2)
    zh = lax.rem(lax.div(ctx, 2), zhs)
    y = lax.div(ctx, 2 * zhs)
    z = zh * zls + zl
    parity = lax.rem(zl, 2)
    me, mate = x * 2 + parity, x * 2 + 1 - parity

    def at(x_to, y_to, z_to, core_to):
        zh_to, zl_to = lax.div(z_to, zls), lax.rem(z_to, zls)
        return {"head": x_to * zls + zl_to, "ctx": (y_to * zhs + zh_to) * 2 + core_to}

    def at_x(x_to):
        return at(x_to, y, z, core)

    def at_y(y_to):
        return at(x, y_to, z, core)

    def at_z(z_to):
        return at(x, y, z_to, core)

    sibling = at(x, y, z, 1 - core)
    mate_device = at_z(z + 1 - 2 * parity)

    def remote(src, dst, send, recv, device):
        return pltpu.make_async_remote_copy(
            src_ref=src, dst_ref=dst, send_sem=send, recv_sem=recv,
            device_id=device, device_id_type=MESH,
        )

    def nearest(own, order, size):
        odd = lax.rem(order, 2)
        return lax.rem(
            own + odd * (size - lax.div(order + 1, 2)) + (1 - odd) * lax.div(order, 2), size
        )

    def y_of(order):
        return nearest(y, order, ys)

    def z_of(order):
        return nearest(z, order, zs)

    def head_lanes(index, size):
        return pl.ds(pl.multiple_of(index * size, HD), size)

    barrier = pltpu.get_barrier_semaphore()
    greeted = [sibling]
    greeted += [at_x(lax.rem(x + hop, xs)) for hop in range(1, xs)]
    greeted += [at_y(lax.rem(y + hop, ys)) for hop in range(1, ys)]
    greeted += [at_z(lax.rem(z + hop, zs)) for hop in range(1, zs)]
    for device in greeted:
        pl.semaphore_signal(barrier, inc=1, device_id=device, device_id_type=MESH)
    pl.semaphore_wait(barrier, len(greeted))

    def key_z(peer, slot):
        return remote(
            key_ref.at[:, :, head_lanes(lax.rem(peer, 2), HD)], key_all.at[y, core, slot],
            kz_ss.at[peer], kz_rs.at[slot], at_z(peer),
        )

    def value_y(peer, slot):
        return remote(
            value_ref, value_stage.at[slot], vy_ss.at[peer], vy_rs.at[slot], at_y(peer)
        )

    query_refs = ((query_ref, query_all), (grad_ref, grad_all))

    def query_pair(part, slot):
        ref, dst = query_refs[part]
        return remote(
            ref.at[:, :, head_lanes(1 - parity, width)], dst.at[slot],
            q_ss.at[part, x], q_rs.at[part, slot], mate_device,
        )

    def query_own(part, x_to, slot):
        ref, dst = query_refs[part]
        return remote(
            ref.at[:, :, head_lanes(parity, width)], dst.at[slot],
            q_ss.at[part, x_to], q_rs.at[part, slot], at_x(x_to),
        )

    def query_mate(part, x_to, slot):
        dst = query_refs[part][1]
        return remote(
            dst.at[mate], dst.at[slot],
            q_ss.at[part, xs + x_to], q_rs.at[part, slot], at_x(x_to),
        )

    for order in reversed(range(1, zs)):
        key_z(z_of(order), z).start()
    for order in reversed(range(1, ys)):
        value_y(y_of(order), y).start()
    for part in range(2):
        query_pair(part, me).start()
    for part in range(2):
        for hop in sorted(range(1, xs), key=lambda h: -min(h, xs - h)):
            query_own(part, lax.rem(x + hop, xs), me).start()
    own = [
        pltpu.make_async_copy(
            key_ref.at[:, :, head_lanes(parity, HD)], key_all.at[y, core, z], local_sem.at[0]
        ),
        pltpu.make_async_copy(value_ref, value_stage.at[y], local_sem.at[1]),
    ]
    own += [
        pltpu.make_async_copy(
            ref.at[:, :, head_lanes(parity, width)], dst.at[me], local_sem.at[2 + part]
        )
        for part, (ref, dst) in enumerate(query_refs)
    ]
    for copy in own:
        copy.start()

    row_of = lax.broadcasted_iota(jnp.int32, (ROWS, toks), 0)

    def fill_positions(y_at, carry):
        for core_at in range(2):
            for z_at in range(zs):
                for half in range(2):
                    block = ((y_at * zhs + z_at // zls) * 2 + core_at) * 2 + half
                    first = order_ref[block] * block_len + (x * zls + z_at % zls) * ROWS
                    group = (core_at * zs + z_at) * 2 + half
                    key_pos[y_at, group * ROWS:(group + 1) * ROWS, :] = row_of + first
        return carry

    lax.fori_loop(0, ys, fill_positions, 0)
    token = lax.broadcasted_iota(jnp.int32, (1, toks), 1)
    half_of = lax.rem(lax.div(token, ROWS), 2)
    pair_of = lax.rem(lax.div(token, 2 * ROWS), 2)
    x_of = lax.div(token, 4 * ROWS)
    block_pos = jnp.where(half_of == 0, order_ref[ctx * 2], order_ref[ctx * 2 + 1])
    query_pos = (
        block_pos * block_len
        + (x_of * zls + (zl - parity) + pair_of) * ROWS
        + lax.rem(token, ROWS)
    )
    attended_acc[...] = jnp.zeros_like(attended_acc)
    query_acc[...] = jnp.zeros_like(query_acc)

    def key_y(peer, slot):
        return remote(
            key_all.at[slot, core], key_all.at[slot, core],
            ky_ss.at[peer], ky_rs.at[slot], at_y(peer),
        )

    def value_z(peer, slot):
        return remote(
            value_stage.at[:, :, :, head_lanes(lax.rem(peer, 2), HD)],
            value_all.at[:, core, slot], vz_ss.at[peer], vz_rs.at[slot], at_z(peer),
        )

    def key_sibling(y_at, core_at):
        ref = key_all.at[y_at, core_at]
        return remote(ref, ref, sk_ss.at[y_at], sk_rs.at[y_at], sibling)

    def value_sibling(z_at, core_at):
        ref = value_all.at[:, core_at, z_at]
        return remote(ref, ref, sv_ss.at[z_at], sv_rs.at[z_at], sibling)

    for copy in own:
        copy.wait()
    for order in range(1, zs):
        key_z(z, z_of(order)).wait_recv()
    for order in range(1, ys):
        key_y(y_of(order), y).start()
    key_sibling(y, core).start()
    for order in range(1, ys):
        value_y(y, y_of(order)).wait_recv()
    for order in range(1, zs):
        value_z(z_of(order), z).start()
    own_value = pltpu.make_async_copy(
        value_stage.at[:, :, :, head_lanes(parity, HD)], value_all.at[:, core, z],
        local_sem.at[4],
    )
    own_value.start()
    for part in range(2):
        query_pair(part, mate).wait_recv()
        for hop in sorted(range(1, xs), key=lambda h: -min(h, xs - h)):
            query_mate(part, lax.rem(x + hop, xs), mate).start()
    own_value.wait()
    value_sibling(z, core).start()
    for part in range(2):
        for hop in range(1, xs):
            other = lax.rem(x + hop, xs)
            query_own(part, x, other * 2 + parity).wait_recv()
            query_mate(part, x, other * 2 + 1 - parity).wait_recv()
    for head_at in range(GROUP):
        lanes = slice(head_at * HD, (head_at + 1) * HD)
        rows = slice(head_at * toks, (head_at + 1) * toks)
        for src, by_row, by_col in (
            (query_all, query_rows, query_cols), (grad_all, grad_rows, grad_cols)
        ):
            tile = src[:, :, :, lanes].astype(F32).reshape(toks, HD)
            by_row[rows, :] = tile.astype(BF16)
            by_col[:, rows] = tile.T.astype(BF16)

    def pass_key(order):
        y_at = y_of(order)
        key_y(y, y_at).wait_recv()
        key_sibling(y_at, core).start()

    def pass_value(order):
        z_at = z_of(order)
        value_z(z, z_at).wait_recv()
        value_sibling(z_at, core).start()

    def score(order, carry):
        @pl.when(order + AHEAD < ys)
        def _():
            pass_key(order + AHEAD)

        @pl.when(order + AHEAD < zs)
        def _():
            pass_value(order + AHEAD)

        y_at = y_of(order)
        key_sibling(y_at, 1 - core).wait_recv()
        key_wide = key_all[y_at].astype(F32).reshape(keys, HD)
        key_cols[y_at] = key_wide.T.astype(BF16)
        key_tile = key_wide.astype(BF16)
        allowed = jnp.concatenate([key_pos[y_at]] * (step // toks), axis=1) <= jnp.concatenate(
            [query_pos] * (step // toks), axis=1
        )
        for first in range(0, cols, step):
            lanes = slice(first, first + step)
            scores = jnp.where(allowed, matmul(key_tile, query_cols[:, lanes]), LOWEST)
            top = jnp.max(scores, axis=0, keepdims=True)
            exp_tile = jnp.exp2((scores - top) * exp_scale)
            exps[y_at, :, lanes] = exp_tile
            exps_low[y_at, :, lanes] = exp_tile.astype(BF16)
            max_rows[pl.ds(y_at, 1), lanes] = top
            sum_rows[pl.ds(y_at, 1), lanes] = jnp.sum(exp_tile, axis=0, keepdims=True)
        return carry

    for order in range(1, AHEAD):
        pass_key(jnp.int32(order))
        pass_value(jnp.int32(order))
    lax.fori_loop(0, ys, score, 0)
    for order in range(ys + AHEAD, zs):
        pass_value(order)
    top = jnp.max(max_rows[...], axis=0, keepdims=True)
    factor = jnp.exp2((max_rows[...] - top) * exp_scale)
    ratio_rows[...] = factor
    scale_row[...] = top
    total = jnp.sum(sum_rows[...] * factor, axis=0, keepdims=True)
    for order in range(zs):
        value_sibling(z_of(order), 1 - core).wait_recv()

    def attend(y_at, carry):
        value_cols = value_all[y_at].astype(F32).reshape(keys, HD).T.astype(BF16)
        for first in range(0, cols, step):
            lanes = slice(first, first + step)
            attended_acc[:, lanes] += (
                matmul(value_cols, exps_low[y_at, :, lanes]) * ratio_rows[pl.ds(y_at, 1), lanes]
            )
        return carry

    lax.fori_loop(0, ys, attend, 0)

    dots = jnp.sum(attended_acc[...] * grad_cols[...].astype(F32), axis=0, keepdims=True)
    for index, row in enumerate((top, total, dots)):
        for head_at in range(GROUP):
            stat_all[x, index, head_at:head_at + 1, :] = row[
                :, head_at * toks:(head_at + 1) * toks
            ]

    def stat_copy(peer, slot):
        return remote(
            stat_all.at[slot], stat_all.at[slot], stat_ss.at[peer], stat_rs.at[slot], at_x(peer)
        )

    for hop in range(1, xs):
        stat_copy(lax.rem(x + hop, xs), x).start()

    for order in range(zs):
        peer = z_of(order)
        value_sibling(peer, core).wait_send()
        if order:
            key_z(peer, z).wait_send()
            value_z(peer, z).wait_send()
    for order in range(ys):
        peer = y_of(order)
        key_sibling(peer, core).wait_send()
        if order:
            value_y(peer, y).wait_send()
            key_y(peer, y).wait_send()
    for part in range(2):
        query_pair(part, me).wait_send()
        for hop in range(1, xs):
            query_own(part, lax.rem(x + hop, xs), me).wait_send()
            query_mate(part, lax.rem(x + hop, xs), mate).wait_send()

    def weigh(y_at, carry):
        value_tile = value_all[y_at].astype(F32).reshape(keys, HD).astype(BF16)
        for first in range(0, cols, step):
            lanes = slice(first, first + step)
            grad_weights[y_at, :, lanes] = matmul(value_tile, grad_cols[:, lanes])
        return carry

    lax.fori_loop(0, ys, weigh, 0)

    for hop in range(1, xs):
        stat_copy(x, lax.rem(x + hop, xs)).wait_recv()
        stat_copy(lax.rem(x + hop, xs), x).wait_send()
    tops = [stat_all[x_at, 0] for x_at in range(xs)]
    top = functools.reduce(jnp.maximum, tops)
    factors = [jnp.exp2((part - top) * exp_scale) for part in tops]
    total = sum(stat_all[x_at, 1] * factors[x_at] for x_at in range(xs))
    inverse = 1.0 / total
    delta = sum(stat_all[x_at, 2] * factors[x_at] for x_at in range(xs)) * inverse
    for head_at in range(GROUP):
        lanes = slice(head_at * toks, (head_at + 1) * toks)
        row = slice(head_at, head_at + 1)
        delta_row[:, lanes] = delta[row]
        scale_row[:, lanes] = (
            jnp.exp2((scale_row[:, lanes] - top[row]) * exp_scale) * inverse[row]
        )
        ratio_rows[:, lanes] = (
            jnp.exp2((max_rows[:, lanes] - top[row]) * exp_scale) * inverse[row]
        )

    def out_x(part, peer, slot):
        return remote(
            out_part.at[part, peer], out_in.at[part, slot],
            ox_ss.at[part, peer], ox_rs.at[part, slot], at_x(peer),
        )

    def out_pair(part):
        return remote(
            pair_send.at[part], pair_in.at[part], oz_ss.at[part], oz_rs.at[part], mate_device
        )

    def send_out(part, acc, scale):
        for head_at in range(GROUP):
            lanes = slice(head_at * HD, (head_at + 1) * HD)
            rows = slice(head_at * toks, (head_at + 1) * toks)
            out_part[part, :, :, :, :, lanes] = (
                (acc[:, rows] * scale(rows)).T.reshape(xs, 2, 2, ROWS, HD).astype(BF16)
            )
        for hop in sorted(range(1, xs), key=lambda h: -min(h, xs - h)):
            out_x(part, lax.rem(x + hop, xs), x).start()
        out_in[part, x] = out_part[part, x]

    def add_out(part, out):
        for hop in range(1, xs):
            out_x(part, x, lax.rem(x + hop, xs)).wait_recv()
        pair_send[part] = sum(
            out_in[part, x_at, 1 - parity].astype(F32) for x_at in range(xs)
        ).astype(BF16)
        out_pair(part).start()
        out[:, :, head_lanes(parity, width)] = sum(
            out_in[part, x_at, parity].astype(F32) for x_at in range(xs)
        ).astype(BF16)

    send_out(0, attended_acc, lambda rows: scale_row[:, rows])

    def dsib_copy(order, core_at):
        return remote(
            kv_part.at[order, core_at], sibling_in.at[order],
            dsib_ss.at[order], dsib_rs.at[order], sibling,
        )

    def dkey_y(order):
        return remote(
            key_send.at[order], key_in.at[order],
            dky_ss.at[order], dky_rs.at[order], at_y(y_of(order)),
        )

    def dvalue_z(order, peer, slot):
        return remote(
            value_send.at[peer, order], value_in.at[slot, order],
            dvz_ss.at[peer], dvz_rs.at[slot], at_z(peer),
        )

    def dvalue_all(peer, slot):
        return remote(
            value_send.at[peer], value_in.at[slot], dvz_ss.at[peer], dvz_rs.at[slot], at_z(peer)
        )

    def add_sibling(order):
        dsib_copy(order, 1 - core).wait_recv()
        key_send[order] = (
            kv_part[order, core, 0].astype(F32) + sibling_in[order, 0].astype(F32)
        ).astype(BF16)
        value_send[:, order] = (
            kv_part[order, core, 1].astype(F32) + sibling_in[order, 1].astype(F32)
        ).astype(BF16)
        for near in reversed(range(1, zs)):
            dvalue_z(order, z_of(near), z).start()

    def backward(turn, carry):
        order = ys - 1 - turn
        y_at = y_of(order)
        key_sum = jnp.zeros((keys, HD), F32)
        value_sum = jnp.zeros((keys, HD), F32)
        for first in range(0, cols, step):
            lanes = slice(first, first + step)
            probs = exps[y_at, :, lanes] * ratio_rows[pl.ds(y_at, 1), lanes]
            weights = probs.astype(BF16)
            grad_scores = (
                probs * (grad_weights[y_at, :, lanes] - delta_row[:, lanes])
            ).astype(BF16)
            query_acc[:, lanes] += matmul(key_cols[y_at], grad_scores)
            value_sum += matmul(weights, grad_rows[lanes, :])
            key_sum += matmul(grad_scores, query_rows[lanes, :])
        shape = (2, zs, 2, ROWS, HD)
        kv_part[order, :, 0] = (key_sum * scaling).reshape(shape).astype(BF16)
        kv_part[order, :, 1] = value_sum.reshape(shape).astype(BF16)
        dsib_copy(order, 1 - core).start()

        @pl.when(turn >= 1)
        def _():
            add_sibling(order + 1)
            dkey_y(order + 1).start()

        return carry

    lax.fori_loop(0, ys, backward, 0)

    send_out(1, query_acc, lambda rows: scaling)
    add_out(0, attended_out)
    add_sibling(0)
    value_in[z] = value_send[z]

    total_key = key_send[0].astype(F32)
    for order in range(1, ys):
        dkey_y(order).wait_recv()
        total_key += key_in[order].astype(F32)
    key_last[...] = total_key.astype(BF16)

    def dkey_z(peer, slot):
        return remote(
            key_last.at[peer], key_home.at[slot], dkz_ss.at[peer], dkz_rs.at[slot], at_z(peer)
        )

    def dvalue_y(order):
        return remote(
            value_last.at[order], value_home.at[order],
            dvy_ss.at[order], dvy_rs.at[order], at_y(y_of(order)),
        )

    for near in reversed(range(1, zs)):
        dkey_z(z_of(near), z).start()
    key_home[z] = key_last[z]
    for near in range(1, zs):
        dvalue_all(z, z_of(near)).wait_recv()
    for half in range(2):
        value_last[:, half] = sum(
            value_in[z_at].astype(F32) for z_at in range(half, zs, 2)
        ).astype(BF16)
    for order in reversed(range(1, ys)):
        dvalue_y(order).start()
    value_home[0] = value_last[0]

    for order in range(ys):
        dsib_copy(order, 1 - core).wait_send()
        if order:
            dkey_y(order).wait_send()
    for order in range(1, zs):
        dvalue_all(z_of(order), z).wait_send()
    add_out(1, query_out)
    for part in range(2):
        for hop in range(1, xs):
            out_x(part, lax.rem(x + hop, xs), x).wait_send()
    for near in range(1, zs):
        dkey_z(z, z_of(near)).wait_recv()
    for half in range(2):
        key_out[:, :, half * HD:(half + 1) * HD] = sum(
            key_home[z_at].astype(F32) for z_at in range(half, zs, 2)
        ).astype(BF16)
    for order in range(1, ys):
        dvalue_y(order).wait_recv()
    for half in range(2):
        value_out[:, :, half * HD:(half + 1) * HD] = sum(
            value_home[order, half].astype(F32) for order in range(ys)
        ).astype(BF16)
    for part, out in enumerate((attended_out, query_out)):
        out_pair(part).wait_recv()
        out[:, :, head_lanes(1 - parity, width)] = pair_in[part]

    for order in range(1, zs):
        dkey_z(z_of(order), z).wait_send()
    for order in range(1, ys):
        dvalue_y(order).wait_send()
    for part in range(2):
        out_pair(part).wait_send()


def finish(*refs):
    for src, dst in zip(refs[:4], refs[4:]):
        dst[...] = src[...]


def shards(split, queries, key_vectors, value_vectors, out_grad, block_order):
    xs, zls, ys, zhs = split["x"], split["z_lo"], split["y"], split["z_hi"]
    zs, srcs = zls * zhs, 2 * xs
    toks = srcs * 2 * ROWS
    cols = GROUP * toks
    keys = 2 * zs * 2 * ROWS
    width = GROUP * HD
    vmem = pltpu.VMEM
    dma = pltpu.SemaphoreType.DMA
    tile = (2, ROWS, HD)
    whole = pl.BlockSpec(memory_space=pltpu.VMEM)
    results = tuple(
        jax.ShapeDtypeStruct(a.shape, BF16)
        for a in (queries, queries, key_vectors, value_vectors)
    )
    partial_sums = pl.pallas_call(
        functools.partial(kernel, split),
        out_shape=results,
        in_specs=[pl.BlockSpec(memory_space=pl.ANY)] * 4
        + [pl.BlockSpec(memory_space=pltpu.SMEM)],
        out_specs=(whole,) * 4,
        scratch_shapes=[
            vmem((srcs, 2, ROWS, width), BF16), vmem((srcs, 2, ROWS, width), BF16),
            vmem((ys, 2, zs) + tile, BF16), vmem((ys, 2, zs) + tile, BF16),
            vmem((ys,) + value_vectors.shape, BF16),
            vmem((cols, HD), BF16), vmem((cols, HD), BF16),
            vmem((HD, cols), BF16), vmem((HD, cols), BF16),
            vmem((ys, HD, keys), BF16),
            vmem((ys, keys, toks), jnp.int32),
            vmem((ys, keys, cols), F32), vmem((ys, keys, cols), BF16),
            vmem((ys, keys, cols), F32),
            vmem((ys, cols), F32), vmem((ys, cols), F32), vmem((ys, cols), F32), vmem((1, cols), F32), vmem((1, cols), F32),
            vmem((xs, 3, GROUP, toks), F32),
            vmem((HD, cols), F32), vmem((HD, cols), F32),
            vmem((2, xs, 2, 2, ROWS, width), BF16), vmem((2, xs, 2, 2, ROWS, width), BF16),
            vmem((2, 2, ROWS, width), BF16), vmem((2, 2, ROWS, width), BF16),
            vmem((ys, 2, 2, zs) + tile, BF16), vmem((ys, 2, zs) + tile, BF16),
            vmem((ys, zs) + tile, BF16), vmem((ys, zs) + tile, BF16),
            vmem((zs, ys) + tile, BF16), vmem((zs, ys) + tile, BF16),
            vmem((zs,) + tile, BF16), vmem((zs,) + tile, BF16),
            vmem((ys, 2) + tile, BF16), vmem((ys, 2) + tile, BF16),
            dma((2, 2 * xs)), dma((2, srcs)), dma((zs,)), dma((zs,)), dma((ys,)), dma((ys,)),
            dma((ys,)), dma((ys,)), dma((zs,)), dma((zs,)),
            dma((ys,)), dma((ys,)), dma((zs,)), dma((zs,)), dma((xs,)), dma((xs,)),
            dma((ys,)), dma((ys,)),
            dma((ys,)), dma((ys,)), dma((zs,)), dma((zs,)),
            dma((zs,)), dma((zs,)), dma((ys,)), dma((ys,)),
            dma((2, xs)), dma((2, xs)), dma((2,)), dma((2,)), dma((5,)),
        ],
        compiler_params=pltpu.CompilerParams(
            collective_id=0, has_side_effects=True, vmem_limit_bytes=56 * 1024 * 1024
        ),
        name="attention",
    )(queries, out_grad, key_vectors, value_vectors, block_order)
    return pl.pallas_call(
        finish, out_shape=results, in_specs=[whole] * 4, out_specs=(whole,) * 4, name="finish"
    )(*partial_sums)


def solution(mesh, split=SPLIT):
    rows = P("ctx", "head", None)
    return jax.shard_map(
        functools.partial(shards, split),
        mesh=mesh,
        in_specs=(rows, rows, rows, rows, P()),
        out_specs=(rows,) * 4,
        check_vma=False,
    )
```
